128 devices in a mesh: depth: 8 (over x_lo, z), probe: 16 (over x_hi, y, core).
Axes of the slice: x: 4 (x_hi: 2, x_lo: 2; x = x_hi * 2 + x_lo), y: 4, z: 4, core: 2. Of those that a mesh axis runs over, the one named last changes fastest.
Arguments:
- residual: bfloat16 [64, 2, 256, 256], P('probe'), may hold values from -4 to 4
- saved_waves: bfloat16 [16, 64, 2, 256, 256], P('depth', 'probe'), may hold values from -4 to 4
- object_phase: float32 [16, 384, 384], P('depth'), may hold values from -3.140625 to 3.140625
- object_amp: float32 [16, 384, 384], P('depth'), may hold values from 0.25 to 1.75
- prop_phase: float32 [256, 256], replicated, may hold values from -3.140625 to 3.140625
- offsets: int32 [64, 2], P('probe'), may hold values from 0 to 128
Outputs:
- object_grad: float32 [16, 2, 384, 384], P('depth', None, 'probe')
- probe_grad: float32 [2, 256, 256], P(None, 'probe', 'depth')
The draws below stay inside these ranges and needn't reach their ends.
Inputs may be any that keep to these rules, and one draw needn't show every extreme that they name: `offsets`: every window lies inside the patch.
All inputs are finite; a program needn't handle non-finite values.
Results may differ from the reference program's by a relative error of at most 0.025.
The reference program's roundings to bfloat16 on the way (of `chi`) count: a program that leaves them out, or rounds other values in their place, can miss the bound.
Values may be sent and summed in bfloat16 or wider, within the bound.
No kernel may reach another device: no remote copies, remote signals or barrier semaphores. Data moves between devices by JAX's collectives and lax.ppermute only.
A program may use at most 128 MiB of HBM per device.

```python
import math
import jax
import jax.numpy as jnp
from jax import lax

M = 256
PATCH = 384
SLICES = 16
POSITIONS = 64


def set_ends(values, key, least, high):
    dims = values.shape
    spot = [jax.random.randint(jax.random.fold_in(key, axis), (), 0, dims[axis]) for axis in range(len(dims))]
    values = values.at[tuple(spot)].set(least)
    longest = dims.index(max(dims))
    spot[longest] = (spot[longest] + 1) % dims[longest]
    return values.at[tuple(spot)].set(high)


def shard_levels(stream_key, extent, cuts, low, top_value):
    gain, own = 1.0, jax.random.fold_in(stream_key, 6)
    for axis_at, blocks in cuts:
        heights = jnp.exp(jax.random.uniform(jax.random.fold_in(own, axis_at), (blocks,), jnp.float32, low / len(cuts), top_value / len(cuts)))
        gain = gain * jnp.repeat(heights, extent[axis_at] // blocks).reshape([-1 if axis == axis_at else 1 for axis in range(len(extent))])
    return gain


def centred(key, dims, scale, reach, split=(), kind=jnp.bfloat16):
    values = jax.random.normal(key, dims, jnp.float32) * scale
    if len(split) > 0:
        values = shard_levels(key, dims, split, -0.22, 0.18) * values
    return jnp.clip(values, min=-reach, max=reach).astype(kind)


def setup_inputs(seed: int = 0) -> dict:
    arg_keys = jax.random.split(jax.random.key(seed), 7)
    residual = centred(arg_keys[0], (POSITIONS, 2, M, M), 0.25, 4.0, ((0, 16),))
    saved_waves = centred(arg_keys[1], (SLICES, POSITIONS, 2, M, M), 0.3, 4.0, ((0, 8), (1, 16)))
    object_phase = jnp.clip(jax.random.uniform(arg_keys[2], (SLICES, PATCH, PATCH), jnp.float32, -3.140625, 3.140625), -3.140625, 3.140625)
    object_amp = jnp.clip(1.0 + 0.15 * jax.random.normal(arg_keys[3], (SLICES, PATCH, PATCH), jnp.float32), 0.25, 1.75)
    prop_phase = jnp.clip(jax.random.uniform(arg_keys[4], (M, M), jnp.float32, -3.140625, 3.140625), -3.140625, 3.140625)
    offsets = set_ends(jax.random.randint(arg_keys[5], (POSITIONS, 2), 0, PATCH - M + 1), jax.random.fold_in(arg_keys[5], 1), 0, PATCH - M).astype(jnp.int32)
    return dict(residual=residual, saved_waves=saved_waves, object_phase=object_phase, object_amp=object_amp, prop_phase=prop_phase, offsets=offsets)


def tables(width):
    rows = lax.broadcasted_iota(jnp.int32, (width, width), 0)
    cols = lax.broadcasted_iota(jnp.int32, (width, width), 1)
    phase = 2.0 * math.pi / width * (rows * cols % width).astype(jnp.float32)
    factor = 1.0 / math.sqrt(width)
    return ((jnp.cos(phase) * factor).astype(jnp.bfloat16), (jnp.sin(phase) * factor).astype(jnp.bfloat16))

def left_apply(real_part, imag_part, waves):
    block = jnp.concatenate([jnp.concatenate([real_part, -imag_part], 1), jnp.concatenate([imag_part, real_part], 1)], 0)
    batch, _, width, _ = waves.shape
    flat = waves.reshape(batch, 2 * width, width)
    result = jnp.einsum('jk,bkl->bjl', block.astype(jnp.float32), flat.astype(jnp.float32), precision=lax.Precision.HIGHEST)
    return result.reshape(batch, 2, width, width)

def right_apply(real_part, imag_part, waves):
    batch, _, width, _ = waves.shape
    real_table = real_part.astype(jnp.float32)
    imag_table = imag_part.astype(jnp.float32)
    wave_real = waves[:, 0].reshape(batch * width, width).astype(jnp.float32)
    wave_imag = waves[:, 1].reshape(batch * width, width).astype(jnp.float32)
    high = lax.Precision.HIGHEST
    out_real = jnp.dot(wave_real, real_table, precision=high) - jnp.dot(wave_imag, imag_table, precision=high)
    out_imag = jnp.dot(wave_real, imag_table, precision=high) + jnp.dot(wave_imag, real_table, precision=high)
    return jnp.stack([out_real, out_imag], 1).reshape(batch, 2, width, width)

def back_propagate(chi, cosine, sine, kernel_cos, kernel_sin):
    first = left_apply(cosine, -sine, chi)
    spectrum = right_apply(cosine, -sine, first)
    spec_real = spectrum[:, 0]
    spec_imag = spectrum[:, 1]
    filtered = jnp.stack([kernel_cos * spec_real + kernel_sin * spec_imag, kernel_cos * spec_imag - kernel_sin * spec_real], 1)
    second = left_apply(cosine, sine, filtered)
    return right_apply(cosine, sine, second)

def reference(residual, saved_waves, object_phase, object_amp, prop_phase, offsets):
    width = residual.shape[-1]
    patch = object_phase.shape[-1]
    slice_count = object_phase.shape[0]
    cosine, sine = tables(width)
    kernel_cos = jnp.cos(prop_phase)
    kernel_sin = jnp.sin(prop_phase)
    trans_real = object_amp * jnp.cos(object_phase)
    trans_imag = object_amp * jnp.sin(object_phase)
    zero_index = jnp.zeros((), jnp.int32)

    def visit(carry, index):
        grads, probe_total = carry
        chi = lax.dynamic_index_in_dim(residual, index, 0, keepdims=True)
        row_start = offsets[index, 0].astype(jnp.int32)
        col_start = offsets[index, 1].astype(jnp.int32)
        for layer in range(slice_count - 1, -1, -1):
            arrived = back_propagate(chi, cosine, sine, kernel_cos, kernel_sin)[0]
            chi_real = arrived[0]
            chi_imag = arrived[1]
            wave = lax.dynamic_index_in_dim(saved_waves[layer], index, 0, keepdims=False).astype(jnp.float32)
            psi_real = wave[0]
            psi_imag = wave[1]
            term = jnp.stack([psi_real * chi_real + psi_imag * chi_imag, psi_real * chi_imag - psi_imag * chi_real])
            layer_grad = grads[layer]
            window = lax.dynamic_slice(layer_grad, (zero_index, row_start, col_start), (2, width, width))
            layer_grad = lax.dynamic_update_slice(layer_grad, window + term, (zero_index, row_start, col_start))
            grads = grads.at[layer].set(layer_grad)
            tr = lax.dynamic_slice(trans_real[layer], (row_start, col_start), (width, width))
            ti = lax.dynamic_slice(trans_imag[layer], (row_start, col_start), (width, width))
            chi = jnp.stack([tr * chi_real + ti * chi_imag, tr * chi_imag - ti * chi_real])[None].astype(jnp.bfloat16)
        probe_total = probe_total + chi[0].astype(jnp.float32)
        return ((grads, probe_total), None)
    start_grads = jnp.zeros((slice_count, 2, patch, patch), jnp.float32)
    start_probe = jnp.zeros((2, width, width), jnp.float32)
    indices = jnp.arange(residual.shape[0], dtype=jnp.int32)
    (grads, probe_total), _ = lax.scan(visit, (start_grads, start_probe), indices)
    return (grads, probe_total)
```

```python
import functools
import math

import jax
import jax.numpy as jnp
from jax import lax
from jax.experimental import pallas as pl
from jax.experimental.pallas import tpu as pltpu
from jax.sharding import PartitionSpec as P

BF = jnp.bfloat16
F32 = jnp.float32
RING = 4
N = 256
HALF = 128
PATCH = 384
ANY = pl.BlockSpec(memory_space=pl.ANY)
VM = pl.BlockSpec(memory_space=pltpu.VMEM)
SM = pl.BlockSpec(memory_space=pltpu.SMEM)
VMEM_LIMIT = 48 * 1024 * 1024


def half(index):
    return slice(index * HALF, (index + 1) * HALF)


def transform_tables(width):
    span = width // 2
    shape = (2, width, width)
    parity = lax.broadcasted_iota(jnp.int32, shape, 0)

    def build(spread_dim, sign):
        rows = lax.broadcasted_iota(jnp.int32, shape, 1)
        cols = lax.broadcasted_iota(jnp.int32, shape, 2)
        spread, other = (rows, cols) if spread_dim == 1 else (cols, rows)
        order = (2 * (spread % span) + parity) * (other % span) % width
        phase = 2.0 * math.pi / width * order.astype(F32)
        factor = 1.0 / math.sqrt(width)
        low = rows < span
        left = cols < span
        value = jnp.where(low == left, jnp.cos(phase), jnp.where(low, sign, -sign) * jnp.sin(phase))
        return (value * factor).astype(BF)

    return build(2, 1.0), build(1, 1.0), build(2, -1.0)


def split_order(array):
    span = array.shape[0] // 2
    return array.reshape(span, 2, span, 2).transpose(1, 0, 3, 2).reshape(array.shape)


def dot(a, b):
    return jnp.dot(a, b, preferred_element_type=F32)


def back_step(source, tables, mixed, filtered, second, finish):
    inward, table, flipped, kernel_cos, kernel_sin = tables
    for part in (0, 1):
        even = dot(inward[0, half(part), :], source[0])
        odd = dot(inward[1, half(part), :], source[1])
        for row, value in ((0, even + odd), (1, even - odd)):
            left, right = value[:, :HALF], value[:, HALF:]
            mixed[0, half(row), half(part)] = (left + right).astype(BF)
            mixed[1, half(row), half(part)] = (left - right).astype(BF)
    for col in (0, 1):
        upper = dot(mixed[col, half(0), :], flipped[col])
        lower = dot(mixed[col, half(1), :], flipped[col])
        for parity in (0, 1):
            real = upper[:, half(parity)]
            imag = lower[:, half(parity)]
            kc = kernel_cos[half(parity), half(col)]
            ks = kernel_sin[half(parity), half(col)]
            filtered[parity, half(0), half(col)] = (kc * real + ks * imag).astype(BF)
            filtered[parity, half(1), half(col)] = (kc * imag - ks * real).astype(BF)
    for part in (0, 1):
        even = dot(flipped[0, half(part), :], filtered[0])
        odd = dot(flipped[1, half(part), :], filtered[1])
        total = (even + odd).astype(BF)
        diff = (even - odd).astype(BF)
        for col in (0, 1):
            second[col, half(0), half(part)] = total[:, half(col)]
            second[col, half(1), half(part)] = diff[:, half(col)]
    totals, diffs = [], []
    for row in (0, 1):
        even = dot(second[0, half(row), :], table[0])
        odd = dot(second[1, half(row), :], table[1])
        totals.append(even + odd)
        diffs.append(even - odd)
    for parity in (0, 1):
        finish(
            parity,
            (totals[0][:, half(parity)], diffs[0][:, half(parity)]),
            (totals[1][:, half(parity)], diffs[1][:, half(parity)]),
        )


def step_scratch():
    return [pltpu.VMEM((2, N, N), BF), pltpu.VMEM((2, N, N), BF), pltpu.VMEM((2, N, N), BF)]


def sine_and_cosine(angle):
    half_angle = 0.5 * angle
    square = half_angle * half_angle

    def series(first):
        value = jnp.full_like(square, (-1.0) ** 6 / math.factorial(12 + first))
        for term in range(5, -1, -1):
            value = value * square + (-1.0) ** term / math.factorial(2 * term + first)
        return value

    low_sine = half_angle * series(1)
    low_cosine = series(0)
    return 2.0 * low_sine * low_cosine, 1.0 - 2.0 * low_sine * low_sine


def window_kernel(where, offsets, phase, amp, *rest):
    outs, field = rest[:RING], rest[RING]
    rank = where[0]
    for layer in (0, 1):
        for col in range(3):
            for block in range(3):
                sine, cosine = sine_and_cosine(phase[layer, half(block), half(col)])
                size = amp[layer, half(block), half(col)]
                field[layer, 0, col, half(block), :] = size * cosine
                field[layer, 1, col, half(block), :] = size * sine
    lane = lax.broadcasted_iota(jnp.int32, (HALF, HALF), 1)
    for distance in range(RING):
        position = (rank + distance) % RING
        col_at = offsets[position, 1]
        turn = (HALF - col_at) % HALF
        inside = lane < HALF - col_at
        for parity in (0, 1):
            rows = pl.ds(offsets[position, 0] + parity, HALF, stride=2)
            for layer in (0, 1):
                for part in (0, 1):
                    turned = [
                        pltpu.roll(field[layer, part, col, rows, :], turn, 1) for col in range(3)
                    ]
                    for col in (0, 1):
                        outs[distance][layer, parity, half(part), half(col)] = jnp.where(
                            inside, turned[col], turned[col + 1]
                        ).astype(BF)


def transmission_windows(where, offsets, phase, amp):
    shape = jax.ShapeDtypeStruct((2, 2, N, N), BF)
    return pl.pallas_call(
        window_kernel,
        name="windows",
        out_shape=[shape] * RING,
        in_specs=[SM, SM, VM, VM],
        out_specs=[VM] * RING,
        scratch_shapes=[pltpu.VMEM((2, 2, 3, PATCH, HALF), F32)],
        compiler_params=pltpu.CompilerParams(vmem_limit_bytes=VMEM_LIMIT),
    )(where, offsets, phase, amp)


def chain_kernel(first, where, start, *rest):
    windows = rest[:RING]
    earlier = () if first else rest[RING : 2 * RING]
    rest = rest[RING + len(earlier) :]
    tables = rest[:5]
    count = RING + 1 if first else RING
    outs = rest[5 : 5 + count]
    trans, waves, middle, mixed, filtered, second, in_sems, out_sems = rest[5 + count :]
    rank = where[0]
    active = where[1] == 1 if first else where[1] == 0

    def loads():
        copies = []
        for distance in range(RING):
            slot = (rank + RING - distance) % RING
            copies.append(
                pltpu.make_async_copy(windows[distance], trans.at[slot], in_sems.at[distance])
            )
        copies.append(
            pltpu.make_async_copy(start, waves.at[(2 * RING - 1 - rank) % RING], in_sems.at[RING])
        )
        return copies

    def stores():
        return [
            pltpu.make_async_copy(waves.at[k], outs[k], out_sems.at[k]) for k in range(count)
        ]

    @pl.when(active)
    def _():
        for copy in loads():
            copy.start()
        for copy in loads():
            copy.wait()

        def pair(step, carry):
            pair_at = RING - 1 - step
            source = waves.at[(pair_at + RING - rank) % RING]
            target = waves.at[
                jnp.where(pair_at == 0, RING, (pair_at + 2 * RING - 1 - rank) % RING)
            ]
            for layer, begin, end in ((1, source, middle), (0, middle, target)):

                def finish(parity, reals, imags, layer=layer, end=end):
                    for col in (0, 1):
                        tr = trans[pair_at, layer, parity, half(0), half(col)].astype(F32)
                        ti = trans[pair_at, layer, parity, half(1), half(col)].astype(F32)
                        qr, qi = reals[col], imags[col]
                        end[parity, half(0), half(col)] = (tr * qr + ti * qi).astype(BF)
                        end[parity, half(1), half(col)] = (tr * qi - ti * qr).astype(BF)

                back_step(begin, tables, mixed, filtered, second, finish)
            return carry

        lax.fori_loop(0, RING, pair, 0)
        for copy in stores():
            copy.start()
        for copy in stores():
            copy.wait()

    if not first:

        @pl.when(jnp.logical_not(active))
        def _():
            copies = [
                pltpu.make_async_copy(earlier[k], outs[k], out_sems.at[k]) for k in range(RING)
            ]
            for copy in copies:
                copy.start()
            for copy in copies:
                copy.wait()


def run_chain(first, where, start, windows, earlier, tables):
    count = RING + 1 if first else RING
    wave = jax.ShapeDtypeStruct((2, N, N), BF)
    return pl.pallas_call(
        functools.partial(chain_kernel, first),
        name="chain_deep" if first else "chain_top",
        out_shape=[wave] * count,
        in_specs=[SM, ANY] + [ANY] * RING + [ANY] * len(earlier) + [VM] * 5,
        out_specs=[ANY] * count,
        scratch_shapes=[
            pltpu.VMEM((RING, 2, 2, N, N), BF),
            pltpu.VMEM((RING + 1, 2, N, N), BF),
            pltpu.VMEM((2, N, N), BF),
            *step_scratch(),
            pltpu.SemaphoreType.DMA((RING + 1,)),
            pltpu.SemaphoreType.DMA((RING + 1,)),
        ],
        compiler_params=pltpu.CompilerParams(vmem_limit_bytes=VMEM_LIMIT),
    )(where, start, *windows, *earlier, *tables)


def terms_kernel(where, offsets, saved, *rest):
    windows = rest[:RING]
    entries = rest[RING : 2 * RING]
    tables = rest[2 * RING : 2 * RING + 5]
    payload = rest[2 * RING + 5]
    trans, waves, psi, grads, ending, final, middle, mixed, filtered, second, sems = rest[
        2 * RING + 6 :
    ]
    rank = where[0]

    def loads(index):
        position = (rank + RING - index) % RING
        return [
            pltpu.make_async_copy(entries[index], waves.at[index], sems.at[0, index]),
            pltpu.make_async_copy(
                windows[(RING - index) % RING], trans.at[index], sems.at[1, index]
            ),
            pltpu.make_async_copy(saved.at[position], psi.at[index], sems.at[2, index]),
        ]

    for index in range(RING):
        for copy in loads(index):
            copy.start()
    grads[...] = jnp.zeros_like(grads)
    ending[...] = jnp.zeros_like(ending)
    for index in range(RING):
        for copy in loads(index):
            copy.wait()
    lane = lax.broadcasted_iota(jnp.int32, (HALF, HALF), 1)

    def visit(index, carry):
        position = (rank + RING - index) % RING
        col_at = offsets[position, 1]
        turn = col_at % HALF
        inside = lane >= col_at

        for layer in (1, 0):

            def finish(parity, reals, imags, layer=layer):
                terms = ([], [])
                for col in (0, 1):
                    wr = psi[index, layer, parity, half(0), half(col)].astype(F32)
                    wi = psi[index, layer, parity, half(1), half(col)].astype(F32)
                    tr = trans[index, layer, parity, half(0), half(col)].astype(F32)
                    ti = trans[index, layer, parity, half(1), half(col)].astype(F32)
                    qr, qi = reals[col], imags[col]
                    terms[0].append(pltpu.roll(wr * qr + wi * qi, turn, 1))
                    terms[1].append(pltpu.roll(wr * qi - wi * qr, turn, 1))
                    next_real = (tr * qr + ti * qi).astype(BF)
                    next_imag = (tr * qi - ti * qr).astype(BF)
                    if layer == 1:
                        middle[parity, half(0), half(col)] = next_real
                        middle[parity, half(1), half(col)] = next_imag
                    else:
                        ending[parity, half(0), half(col)] += next_real.astype(F32)
                        ending[parity, half(1), half(col)] += next_imag.astype(F32)
                rows = pl.ds(offsets[position, 0] + parity, HALF, stride=2)
                zero = jnp.zeros((HALF, HALF), F32)
                for part in (0, 1):
                    left, right = terms[part]
                    placed = (
                        jnp.where(inside, left, zero),
                        jnp.where(inside, right, left),
                        jnp.where(inside, zero, right),
                    )
                    for col in range(3):
                        grads[layer, part, col, rows, :] += placed[col]

            begin = waves.at[index] if layer == 1 else middle
            back_step(begin, tables, mixed, filtered, second, finish)
        return carry

    lax.fori_loop(0, RING, visit, 0)
    chunks = payload.shape[0]
    rows_each = PATCH // chunks
    probe_each = N // chunks

    for parity in (0, 1):
        for part in (0, 1):
            for col in (0, 1):
                final[part, col, pl.ds(parity, HALF, stride=2), :] = ending[
                    parity, half(part), half(col)
                ]

    def pack(chunk, carry):
        rows = pl.ds(pl.multiple_of(chunk * rows_each, 8), rows_each)
        probe_rows = pl.ds(pl.multiple_of(chunk * probe_each, 8), probe_each)
        for col in range(3):
            pieces = [grads[layer, part, col, rows, :] for layer in (0, 1) for part in (0, 1)]
            if col < 2:
                pieces += [final[part, col, probe_rows, :] for part in (0, 1)]
            else:
                pieces += [jnp.zeros((2 * probe_each, HALF), F32)]
            payload[chunk, :, half(col)] = jnp.concatenate(pieces, 0).astype(BF)
        return carry

    lax.fori_loop(0, chunks, pack, 0)


def slice_terms(chunks, where, offsets, saved, windows, entries, tables):
    rows = 4 * (PATCH // chunks) + 2 * (N // chunks)
    return pl.pallas_call(
        terms_kernel,
        name="terms",
        out_shape=jax.ShapeDtypeStruct((chunks, rows, PATCH), BF),
        in_specs=[SM, SM, ANY] + [ANY] * (2 * RING) + [VM] * 5,
        out_specs=VM,
        scratch_shapes=[
            pltpu.VMEM((RING, 2, 2, N, N), BF),
            pltpu.VMEM((RING, 2, N, N), BF),
            pltpu.VMEM((RING, 2, 2, N, N), BF),
            pltpu.VMEM((2, 2, 3, PATCH, HALF), F32),
            pltpu.VMEM((2, N, N), F32),
            pltpu.VMEM((2, 2, N, HALF), F32),
            pltpu.VMEM((2, N, N), BF),
            *step_scratch(),
            pltpu.SemaphoreType.DMA((3, RING)),
        ],
        compiler_params=pltpu.CompilerParams(vmem_limit_bytes=VMEM_LIMIT),
    )(where, offsets, saved, *windows, *entries, *tables)


def order_kernel(where, residual, saved, start, waves):
    rows = lax.broadcasted_iota(jnp.int32, (N, N), 0)
    cols = lax.broadcasted_iota(jnp.int32, (N, N), 1)
    take = (cols == 2 * (rows % HALF) + rows // HALF).astype(F32).astype(BF)

    def reorder(source, target):
        for part in (0, 1):
            ordered = dot(take, source[part]).astype(BF)
            for parity in (0, 1):
                target[parity, half(part), :] = ordered[half(parity), :]

    for layer in (0, 1):
        reorder(saved.at[layer, 0], waves.at[0, layer])

    @pl.when(pl.program_id(0) == where[0])
    def _():
        reorder(residual.at[0], start)


def row_parity_first(where, residual, saved):
    wave = (2, N, N)
    return pl.pallas_call(
        order_kernel,
        name="reorder",
        out_shape=[
            jax.ShapeDtypeStruct(wave, BF),
            jax.ShapeDtypeStruct((RING, 2, *wave), BF),
        ],
        grid=(RING,),
        in_specs=[
            SM,
            pl.BlockSpec((1, *wave), lambda i: (i, 0, 0, 0)),
            pl.BlockSpec((2, 1, *wave), lambda i: (0, i, 0, 0, 0)),
        ],
        out_specs=[
            pl.BlockSpec(wave, lambda i: (0, 0, 0)),
            pl.BlockSpec((1, 2, *wave), lambda i: (i, 0, 0, 0, 0)),
        ],
        compiler_params=pltpu.CompilerParams(vmem_limit_bytes=VMEM_LIMIT),
    )(where, residual, saved)


def turned(array, distance):
    route = [
        (RING * ring + i, RING * ring + (i + distance) % RING)
        for ring in range(2)
        for i in range(RING)
    ]
    return lax.ppermute(array, "depth", route)


def exchanged(arrays):
    return [arrays[0]] + [turned(arrays[k], k) for k in range(1, RING)]


def shards(residual, saved_waves, object_phase, object_amp, prop_phase, offsets):
    depth_at = lax.axis_index("depth")
    chunks = lax.axis_size("probe")
    where = jnp.stack([depth_at % RING, depth_at // RING]).astype(jnp.int32)
    own = transmission_windows(where, offsets, object_phase, object_amp)
    ordered = split_order(prop_phase)
    tables = (*transform_tables(N), jnp.cos(ordered), jnp.sin(ordered))
    start, waves = row_parity_first(where, residual, saved_waves)
    foreign = exchanged(own)
    *deep, leaving = run_chain(True, where, start, foreign, (), tables)
    arrived = lax.ppermute(leaving, "depth", [(RING + i, i) for i in range(RING)])
    entries = run_chain(False, where, arrived, foreign, deep, tables)
    payload = slice_terms(chunks, where, offsets, waves, own, exchanged(entries), tables)
    received = lax.all_to_all(payload, "probe", 0, 0, tiled=True)
    total = jnp.sum(received.astype(F32), axis=0)
    rows_each = PATCH // chunks
    object_grad = total[: 4 * rows_each].reshape(2, 2, rows_each, PATCH)
    probe_rows = total[4 * rows_each :, :N].reshape(2, N // chunks, 8, N // 8)
    spread = lax.all_to_all(jnp.moveaxis(probe_rows, 2, 0), "depth", 0, 0, tiled=True)
    return (object_grad, spread[0])


def solution(mesh):
    return jax.shard_map(
        shards,
        mesh=mesh,
        in_specs=(
            P("probe", None, None, None),
            P("depth", "probe", None, None, None),
            P("depth", None, None),
            P("depth", None, None),
            P(),
            P("probe", None),
        ),
        out_specs=(P("depth", None, "probe", None), P(None, "probe", "depth")),
        check_vma=False,
    )
```

```python
import functools
import math

import jax
import jax.numpy as jnp
from jax import lax
from jax.experimental import pallas as pl
from jax.experimental.pallas import tpu as pltpu
from jax.sharding import PartitionSpec as P

BF = jnp.bfloat16
F32 = jnp.float32
RING = 4
DEPTH = 8
N = 256
HALF = 128
PATCH = 384
ANY = pl.BlockSpec(memory_space=pl.ANY)
VM = pl.BlockSpec(memory_space=pltpu.VMEM)
SM = pl.BlockSpec(memory_space=pltpu.SMEM)
HB = pl.BlockSpec(memory_space=pltpu.HBM)
SINE = (0.999999995716, -0.166666579699, 0.00833305061733, -0.000198090463574, 2.60516627618e-06)
COSINE = (0.99999999978, -0.49999999357, 0.0416666362089, -0.00138883608423, 2.47601355058e-05, -2.60510761786e-07)
VMEM_LIMIT = 48 * 1024 * 1024


def half(index):
    return slice(index * HALF, (index + 1) * HALF)


def transform_tables(width):
    span = width // 2
    shape = (2, width, width)
    parity = lax.broadcasted_iota(jnp.int32, shape, 0)

    def build(spread_dim, sign):
        rows = lax.broadcasted_iota(jnp.int32, shape, 1)
        cols = lax.broadcasted_iota(jnp.int32, shape, 2)
        spread, other = (rows, cols) if spread_dim == 1 else (cols, rows)
        order = (2 * (spread % span) + parity) * (other % span) % width
        phase = 2.0 * math.pi / width * order.astype(F32)
        factor = 1.0 / math.sqrt(width)
        low = rows < span
        left = cols < span
        value = jnp.where(low == left, jnp.cos(phase), jnp.where(low, sign, -sign) * jnp.sin(phase))
        return (value * factor).astype(BF)

    return build(2, 1.0), build(1, 1.0), build(2, -1.0)


def dot(a, b):
    return jnp.dot(a, b, preferred_element_type=F32)


def back_step(source, tables, mixed, filtered, second, finish):
    inward, table, flipped, kernel_cos, kernel_sin = tables
    for part in (0, 1):
        even = dot(inward[0, half(part), :], source[0])
        odd = dot(inward[1, half(part), :], source[1])
        for row, value in ((0, even + odd), (1, even - odd)):
            left, right = value[:, :HALF], value[:, HALF:]
            mixed[0, half(row), half(part)] = (left + right).astype(BF)
            mixed[1, half(row), half(part)] = (left - right).astype(BF)
    for col in (0, 1):
        upper = dot(mixed[col, half(0), :], flipped[col])
        lower = dot(mixed[col, half(1), :], flipped[col])
        for parity in (0, 1):
            real = upper[:, half(parity)]
            imag = lower[:, half(parity)]
            kc = kernel_cos[half(parity), half(col)]
            ks = kernel_sin[half(parity), half(col)]
            filtered[parity, half(0), half(col)] = (kc * real + ks * imag).astype(BF)
            filtered[parity, half(1), half(col)] = (kc * imag - ks * real).astype(BF)
    for part in (0, 1):
        even = dot(flipped[0, half(part), :], filtered[0])
        odd = dot(flipped[1, half(part), :], filtered[1])
        total = (even + odd).astype(BF)
        diff = (even - odd).astype(BF)
        for col in (0, 1):
            second[col, half(0), half(part)] = total[:, half(col)]
            second[col, half(1), half(part)] = diff[:, half(col)]
    totals, diffs = [], []
    for row in (0, 1):
        even = dot(second[0, half(row), :], table[0])
        odd = dot(second[1, half(row), :], table[1])
        totals.append(even + odd)
        diffs.append(even - odd)
    for parity in (0, 1):
        finish(
            parity,
            (totals[0][:, half(parity)], diffs[0][:, half(parity)]),
            (totals[1][:, half(parity)], diffs[1][:, half(parity)]),
        )


def step_scratch():
    return [pltpu.VMEM((2, N, N), BF), pltpu.VMEM((2, N, N), BF), pltpu.VMEM((2, N, N), BF)]


def sine_and_cosine(angle):
    half_angle = 0.5 * angle
    square = half_angle * half_angle

    def series(factors):
        value = jnp.full_like(square, factors[-1])
        for factor in factors[-2::-1]:
            value = value * square + factor
        return value

    low_sine = half_angle * series(SINE)
    low_cosine = series(COSINE)
    return 2.0 * low_sine * low_cosine, 1.0 - 2.0 * low_sine * low_sine


def filter_kernel(phase, kernel_cos, kernel_sin, plain):
    rows = lax.broadcasted_iota(jnp.int32, (N, N), 0)
    cols = lax.broadcasted_iota(jnp.int32, (N, N), 1)
    take = (rows == 2 * (cols % HALF) + cols // HALF).astype(F32).astype(BF)
    for col in (0, 1):
        sine, cosine = sine_and_cosine(phase[:, half(col)])
        plain[0, col] = cosine
        plain[1, col] = sine
    for index, out in ((0, kernel_cos), (1, kernel_sin)):
        for parity in (0, 1):
            picked = [plain[index, col, pl.ds(parity, HALF, stride=2), :] for col in (0, 1)]
            rest = jnp.concatenate(picked, 1)
            value = jnp.zeros((HALF, N), F32)
            for _ in range(3):
                term = rest.astype(BF)
                value = value + dot(term, take)
                rest = rest - term.astype(F32)
            out[half(parity), :] = value


def filters(phase):
    shape = jax.ShapeDtypeStruct((N, N), F32)
    return pl.pallas_call(
        filter_kernel,
        name="filters",
        out_shape=[shape, shape],
        scratch_shapes=[pltpu.VMEM((2, 2, N, HALF), F32)],
        compiler_params=pltpu.CompilerParams(vmem_limit_bytes=VMEM_LIMIT),
    )(phase)


def window_kernel(where, offsets, phase_all, amp_all, *rest):
    outs, (field, phase, amp, sems) = rest[:RING], rest[RING:]
    rank = where[0]

    def loads(layer, block):
        rows = half(block)
        return [
            pltpu.make_async_copy(
                source.at[layer, rows, :], target.at[layer, rows, :], sems.at[kind, layer, block]
            )
            for kind, source, target in ((0, phase_all, phase), (1, amp_all, amp))
        ]

    for layer in (0, 1):
        for block in range(3):
            for copy in loads(layer, block):
                copy.start()
    for layer in (0, 1):
        for block in range(3):
            for copy in loads(layer, block):
                copy.wait()
            for col in range(3):
                sine, cosine = sine_and_cosine(phase[layer, half(block), half(col)])
                size = amp[layer, half(block), half(col)]
                field[layer, 0, col, half(block), :] = size * cosine
                field[layer, 1, col, half(block), :] = size * sine
    lane = lax.broadcasted_iota(jnp.int32, (HALF, HALF), 1)
    for distance in range(RING):
        position = (rank + distance) % RING
        col_at = offsets[position, 1]
        turn = (HALF - col_at) % HALF
        inside = lane < HALF - col_at
        for parity in (0, 1):
            rows = pl.ds(offsets[position, 0] + parity, HALF, stride=2)
            for layer in (0, 1):
                for part in (0, 1):
                    turned = [
                        pltpu.roll(field[layer, part, col, rows, :], turn, 1) for col in range(3)
                    ]
                    for col in (0, 1):
                        outs[distance][layer, parity, half(part), half(col)] = jnp.where(
                            inside, turned[col], turned[col + 1]
                        ).astype(BF)


def transmission_windows(where, offsets, phase, amp):
    shape = jax.ShapeDtypeStruct((2, 2, N, N), BF)
    return pl.pallas_call(
        window_kernel,
        name="windows",
        out_shape=[shape] * RING,
        in_specs=[SM, SM, HB, HB],
        out_specs=[VM] * RING,
        scratch_shapes=[
            pltpu.VMEM((2, 2, 3, PATCH, HALF), F32),
            pltpu.VMEM((2, PATCH, PATCH), F32),
            pltpu.VMEM((2, PATCH, PATCH), F32),
            pltpu.SemaphoreType.DMA((2, 2, 3)),
        ],
        compiler_params=pltpu.CompilerParams(vmem_limit_bytes=VMEM_LIMIT),
    )(where, offsets, phase, amp)


def chain_kernel(first, where, start, *rest):
    windows = rest[:RING]
    earlier = () if first else rest[RING : 2 * RING]
    rest = rest[RING + len(earlier) :]
    tables = rest[:5]
    count = RING + 1
    outs = rest[5 : 5 + count]
    trans, waves, middle, mixed, filtered, second, in_sems, out_sems = rest[5 + count :]
    rank = where[0]
    active = where[1] == 1 if first else where[1] == 0

    def loads():
        copies = []
        for distance in range(RING):
            slot = (rank + RING - distance) % RING
            copies.append(
                pltpu.make_async_copy(windows[distance], trans.at[slot], in_sems.at[distance])
            )
        copies.append(
            pltpu.make_async_copy(start, waves.at[(2 * RING - 1 - rank) % RING], in_sems.at[RING])
        )
        return copies

    def stores():
        return [
            pltpu.make_async_copy(waves.at[k], outs[k], out_sems.at[k]) for k in range(count)
        ]

    @pl.when(active)
    def _():
        for copy in loads():
            copy.start()
        for copy in loads():
            copy.wait()

        def pair(step, carry):
            pair_at = RING - 1 - step
            source = waves.at[(pair_at + RING - rank) % RING]
            target = waves.at[
                jnp.where(pair_at == 0, RING, (pair_at + 2 * RING - 1 - rank) % RING)
            ]
            for layer, begin, end in ((1, source, middle), (0, middle, target)):

                def finish(parity, reals, imags, layer=layer, end=end):
                    for col in (0, 1):
                        tr = trans[pair_at, layer, parity, half(0), half(col)].astype(F32)
                        ti = trans[pair_at, layer, parity, half(1), half(col)].astype(F32)
                        qr, qi = reals[col], imags[col]
                        end[parity, half(0), half(col)] = (tr * qr + ti * qi).astype(BF)
                        end[parity, half(1), half(col)] = (tr * qi - ti * qr).astype(BF)

                back_step(begin, tables, mixed, filtered, second, finish)
            return carry

        lax.fori_loop(0, RING, pair, 0)
        for copy in stores():
            copy.start()
        for copy in stores():
            copy.wait()

    if not first:

        @pl.when(jnp.logical_not(active))
        def _():
            copies = [
                pltpu.make_async_copy(earlier[k], outs[k], out_sems.at[k]) for k in range(RING)
            ]
            middle[...] = jnp.zeros_like(middle)
            copies.append(pltpu.make_async_copy(middle, outs[RING], out_sems.at[RING]))
            for copy in copies:
                copy.start()
            for copy in copies:
                copy.wait()


def run_chain(first, where, start, windows, earlier, tables):
    count = RING + 1
    wave = jax.ShapeDtypeStruct((2, N, N), BF)
    return pl.pallas_call(
        functools.partial(chain_kernel, first),
        name="chain_deep" if first else "chain_top",
        out_shape=[wave] * count,
        in_specs=[SM, ANY] + [ANY] * RING + [ANY] * len(earlier) + [VM] * 5,
        out_specs=[ANY] * count,
        scratch_shapes=[
            pltpu.VMEM((RING, 2, 2, N, N), BF),
            pltpu.VMEM((RING + 1, 2, N, N), BF),
            pltpu.VMEM((2, N, N), BF),
            *step_scratch(),
            pltpu.SemaphoreType.DMA((RING + 1,)),
            pltpu.SemaphoreType.DMA((RING + 1,)),
        ],
        compiler_params=pltpu.CompilerParams(vmem_limit_bytes=VMEM_LIMIT),
    )(where, start, *windows, *earlier, *tables)


def terms_kernel(where, offsets, saved, *rest):
    windows = rest[:RING]
    entries = rest[RING : 2 * RING]
    tables = rest[2 * RING : 2 * RING + 5]
    probe, payload = rest[2 * RING + 5 : 2 * RING + 7]
    trans, waves, psi, grads, middle_sum, middle, mixed, filtered, second, sems = rest[
        2 * RING + 7 :
    ]
    rank = where[0]

    def loads(index):
        position = (rank + RING - index) % RING
        return [
            pltpu.make_async_copy(entries[index], waves.at[index], sems.at[0, index]),
            pltpu.make_async_copy(
                windows[(RING - index) % RING], trans.at[index], sems.at[1, index]
            ),
            pltpu.make_async_copy(saved.at[position], psi.at[index], sems.at[2, index]),
        ]

    for index in range(RING):
        for copy in loads(index):
            copy.start()
    grads[...] = jnp.zeros_like(grads)
    for index in range(RING):
        for copy in loads(index):
            copy.wait()
    lane = lax.broadcasted_iota(jnp.int32, (HALF, HALF), 1)

    def visit(index, carry):
        position = (rank + RING - index) % RING
        col_at = offsets[position, 1]
        turn = col_at % HALF
        inside = lane >= col_at

        for layer in (1, 0):

            def finish(parity, reals, imags, layer=layer):
                terms = ([], [])
                for col in (0, 1):
                    wr = psi[index, layer, parity, half(0), half(col)].astype(F32)
                    wi = psi[index, layer, parity, half(1), half(col)].astype(F32)
                    tr = trans[index, layer, parity, half(0), half(col)].astype(F32)
                    ti = trans[index, layer, parity, half(1), half(col)].astype(F32)
                    qr, qi = reals[col], imags[col]
                    terms[0].append(pltpu.roll(wr * qr + wi * qi, turn, 1))
                    terms[1].append(pltpu.roll(wr * qi - wi * qr, turn, 1))
                    if layer == 1:
                        middle[parity, half(0), half(col)] = (tr * qr + ti * qi).astype(BF)
                        middle[parity, half(1), half(col)] = (tr * qi - ti * qr).astype(BF)
                rows = pl.ds(offsets[position, 0] + parity, HALF, stride=2)
                zero = jnp.zeros((HALF, HALF), F32)
                for part in (0, 1):
                    left, right = terms[part]
                    placed = (
                        jnp.where(inside, left, zero),
                        jnp.where(inside, right, left),
                        jnp.where(inside, zero, right),
                    )
                    for col in range(3):
                        grads[layer, part, col, rows, :] += placed[col]

            begin = waves.at[index] if layer == 1 else middle
            back_step(begin, tables, mixed, filtered, second, finish)
        return carry

    lax.fori_loop(0, RING, visit, 0)
    chunks = payload.shape[0]
    rows_each = PATCH // chunks
    whole = 4 * rows_each
    total = jnp.zeros((HALF, HALF), F32)
    for source in range(DEPTH):
        total = total + probe[source].astype(F32)
    middle_sum[...] = total

    def pack(chunk, carry):
        rows = pl.ds(pl.multiple_of(chunk * rows_each, 8), rows_each)
        own = pl.ds(pl.multiple_of(chunk * 8, 8), 8)
        for col in range(3):
            pieces = [grads[layer, part, col, rows, :] for layer in (0, 1) for part in (0, 1)]
            pieces.append(middle_sum[own, :] if col == 0 else jnp.zeros((8, HALF), F32))
            pieces.append(jnp.zeros((8, HALF), F32))
            payload[chunk, :, half(col)] = jnp.concatenate(pieces, 0).astype(BF)
        return carry

    lax.fori_loop(0, chunks, pack, 0)


def slice_terms(chunks, where, offsets, saved, windows, entries, tables, probe):
    rows = 4 * (PATCH // chunks) + 16
    return pl.pallas_call(
        terms_kernel,
        name="terms",
        out_shape=jax.ShapeDtypeStruct((chunks, rows, PATCH), BF),
        in_specs=[SM, SM, ANY] + [ANY] * (2 * RING) + [VM] * 6,
        out_specs=VM,
        scratch_shapes=[
            pltpu.VMEM((RING, 2, 2, N, N), BF),
            pltpu.VMEM((RING, 2, N, N), BF),
            pltpu.VMEM((RING, 2, 2, N, N), BF),
            pltpu.VMEM((2, 2, 3, PATCH, HALF), F32),
            pltpu.VMEM((HALF, HALF), F32),
            pltpu.VMEM((2, N, N), BF),
            *step_scratch(),
            pltpu.SemaphoreType.DMA((3, RING)),
        ],
        compiler_params=pltpu.CompilerParams(vmem_limit_bytes=VMEM_LIMIT),
    )(where, offsets, saved, *windows, *entries, *tables, probe)


def order_kernel(where, residual, saved, start, waves):
    rows = lax.broadcasted_iota(jnp.int32, (N, N), 0)
    cols = lax.broadcasted_iota(jnp.int32, (N, N), 1)
    take = (cols == 2 * (rows % HALF) + rows // HALF).astype(F32).astype(BF)

    def reorder(source, target):
        for part in (0, 1):
            ordered = dot(take, source[part]).astype(BF)
            for parity in (0, 1):
                target[parity, half(part), :] = ordered[half(parity), :]

    for layer in (0, 1):
        reorder(saved.at[layer, 0], waves.at[0, layer])

    @pl.when(pl.program_id(0) == where[0])
    def _():
        reorder(residual.at[0], start)


def row_parity_first(where, residual, saved):
    wave = (2, N, N)
    return pl.pallas_call(
        order_kernel,
        name="reorder",
        out_shape=[
            jax.ShapeDtypeStruct(wave, BF),
            jax.ShapeDtypeStruct((RING, 2, *wave), BF),
        ],
        grid=(RING,),
        in_specs=[
            SM,
            pl.BlockSpec((1, *wave), lambda i: (i, 0, 0, 0)),
            pl.BlockSpec((2, 1, *wave), lambda i: (0, i, 0, 0, 0)),
        ],
        out_specs=[
            pl.BlockSpec(wave, lambda i: (0, 0, 0)),
            pl.BlockSpec((1, 2, *wave), lambda i: (i, 0, 0, 0, 0)),
        ],
        compiler_params=pltpu.CompilerParams(vmem_limit_bytes=VMEM_LIMIT),
    )(where, residual, saved)


def pieces_kernel(wave, pieces):
    width = N // DEPTH
    lane = lax.broadcasted_iota(jnp.int32, (HALF, HALF), 1) // width
    for piece in range(DEPTH):
        per_tile = HALF // width
        value = jnp.zeros((HALF, HALF), F32)
        for parity in (0, 1):
            for part in (0, 1):
                place = 2 * parity + part
                source = wave[parity, half(part), half(piece // per_tile)].astype(F32)
                shift = (place - piece % per_tile) * width % HALF
                moved = pltpu.roll(source, shift, 1) if shift else source
                value = jnp.where(lane == place, moved, value)
        pieces[piece] = value.astype(BF)


def column_pieces(wave):
    return pl.pallas_call(
        pieces_kernel,
        name="pieces",
        out_shape=jax.ShapeDtypeStruct((DEPTH, HALF, HALF), BF),
        compiler_params=pltpu.CompilerParams(vmem_limit_bytes=VMEM_LIMIT),
    )(wave)


def total_kernel(received, rows_out, probe_out):
    chunks, rows, _ = received.shape
    whole = rows - 16
    for at in range(0, rows, 16):
        value = received[0, at : at + 16, :].astype(F32)
        for chunk in range(1, chunks):
            value = value + received[chunk, at : at + 16, :].astype(F32)
        if at < whole:
            rows_out[at : at + 16, :] = value
        else:
            probe_out[...] = value[:8, :HALF]


def totals(received):
    _, rows, _ = received.shape
    return pl.pallas_call(
        total_kernel,
        name="totals",
        out_shape=[
            jax.ShapeDtypeStruct((rows - 16, PATCH), F32),
            jax.ShapeDtypeStruct((8, HALF), F32),
        ],
        compiler_params=pltpu.CompilerParams(vmem_limit_bytes=VMEM_LIMIT),
    )(received)


def turned(array, distance):
    route = [
        (RING * ring + i, RING * ring + (i + distance) % RING)
        for ring in range(2)
        for i in range(RING)
    ]
    return lax.ppermute(array, "depth", route)


def exchanged(arrays):
    return [arrays[0]] + [turned(arrays[k], k) for k in range(1, RING)]


def shards(residual, saved_waves, object_phase, object_amp, prop_phase, offsets):
    depth_at = lax.axis_index("depth")
    chunks = lax.axis_size("probe")
    where = jnp.stack([depth_at % RING, depth_at // RING]).astype(jnp.int32)
    own = transmission_windows(where, offsets, object_phase, object_amp)
    tables = (*transform_tables(N), *filters(prop_phase))
    start, waves = row_parity_first(where, residual, saved_waves)
    foreign = exchanged(own)
    *deep, leaving = run_chain(True, where, start, foreign, (), tables)
    arrived = lax.ppermute(leaving, "depth", [(RING + i, i) for i in range(RING)])
    *entries, ending = run_chain(False, where, arrived, foreign, deep, tables)
    entries = exchanged(entries)
    probe = lax.all_to_all(column_pieces(ending), "depth", 0, 0, tiled=True)
    payload = slice_terms(chunks, where, offsets, waves, own, entries, tables, probe)
    received = lax.all_to_all(payload, "probe", 0, 0, tiled=True)
    rows, probe_rows = totals(received)
    object_grad = rows.reshape(2, 2, PATCH // chunks, PATCH)
    probe_grad = probe_rows.reshape(8, 2, 2, N // DEPTH).transpose(2, 0, 1, 3)
    return (object_grad, probe_grad.reshape(2, 16, N // DEPTH))


def solution(mesh):
    return jax.shard_map(
        shards,
        mesh=mesh,
        in_specs=(
            P("probe", None, None, None),
            P("depth", "probe", None, None, None),
            P("depth", None, None),
            P("depth", None, None),
            P(),
            P("probe", None),
        ),
        out_specs=(P("depth", None, "probe", None), P(None, "probe", "depth")),
        check_vma=False,
    )
```

```python
import functools
import math

import jax
import jax.numpy as jnp
from jax import lax
from jax.experimental import pallas as pl
from jax.experimental.pallas import tpu as pltpu
from jax.sharding import PartitionSpec as P

BF = jnp.bfloat16
F32 = jnp.float32
RING = 4
DEPTH = 8
N = 256
HALF = 128
PATCH = 384
ANY = pl.BlockSpec(memory_space=pl.ANY)
VM = pl.BlockSpec(memory_space=pltpu.VMEM)
SM = pl.BlockSpec(memory_space=pltpu.SMEM)
SINE = (0.999999995716, -0.166666579699, 0.00833305061733, -0.000198090463574, 2.60516627618e-06)
COSINE = (0.99999999978, -0.49999999357, 0.0416666362089, -0.00138883608423, 2.47601355058e-05, -2.60510761786e-07)
VMEM_LIMIT = 20 * 1024 * 1024


def half(index):
    return slice(index * HALF, (index + 1) * HALF)


def transform_tables(width):
    span = width // 2
    shape = (2, width, width)
    parity = lax.broadcasted_iota(jnp.int32, shape, 0)

    def build(spread_dim, sign):
        rows = lax.broadcasted_iota(jnp.int32, shape, 1)
        cols = lax.broadcasted_iota(jnp.int32, shape, 2)
        spread, other = (rows, cols) if spread_dim == 1 else (cols, rows)
        order = (2 * (spread % span) + parity) * (other % span) % width
        phase = 2.0 * math.pi / width * order.astype(F32)
        factor = 1.0 / math.sqrt(width)
        low = rows < span
        left = cols < span
        value = jnp.where(low == left, jnp.cos(phase), jnp.where(low, sign, -sign) * jnp.sin(phase))
        return (value * factor).astype(BF)

    return build(2, 1.0), build(1, 1.0), build(2, -1.0)


def dot(a, b):
    return jnp.dot(a, b, preferred_element_type=F32)


def back_step(source, tables, mixed, filtered, second, finish, ready=None):
    inward, table, flipped, kernel_cos, kernel_sin = tables
    for part in (0, 1):
        even = dot(inward[0, half(part), :], source[0])
        odd = dot(inward[1, half(part), :], source[1])
        for row, value in ((0, even + odd), (1, even - odd)):
            left, right = value[:, :HALF], value[:, HALF:]
            mixed[0, half(row), half(part)] = (left + right).astype(BF)
            mixed[1, half(row), half(part)] = (left - right).astype(BF)
    for col in (0, 1):
        upper = dot(mixed[col, half(0), :], flipped[col])
        lower = dot(mixed[col, half(1), :], flipped[col])
        for parity in (0, 1):
            real = upper[:, half(parity)]
            imag = lower[:, half(parity)]
            kc = kernel_cos[half(parity), half(col)]
            ks = kernel_sin[half(parity), half(col)]
            filtered[parity, half(0), half(col)] = (kc * real + ks * imag).astype(BF)
            filtered[parity, half(1), half(col)] = (kc * imag - ks * real).astype(BF)
    for part in (0, 1):
        even = dot(flipped[0, half(part), :], filtered[0])
        odd = dot(flipped[1, half(part), :], filtered[1])
        total = (even + odd).astype(BF)
        diff = (even - odd).astype(BF)
        for col in (0, 1):
            second[col, half(0), half(part)] = total[:, half(col)]
            second[col, half(1), half(part)] = diff[:, half(col)]
    if ready is not None:
        ready()
    totals, diffs = [], []
    for row in (0, 1):
        even = dot(second[0, half(row), :], table[0])
        odd = dot(second[1, half(row), :], table[1])
        totals.append(even + odd)
        diffs.append(even - odd)
    for parity in (0, 1):
        finish(
            parity,
            (totals[0][:, half(parity)], diffs[0][:, half(parity)]),
            (totals[1][:, half(parity)], diffs[1][:, half(parity)]),
        )


def step_scratch():
    return [pltpu.VMEM((2, N, N), BF), pltpu.VMEM((2, N, N), BF), pltpu.VMEM((2, N, N), BF)]


def sine_and_cosine(angle):
    half_angle = 0.5 * angle
    square = half_angle * half_angle

    def series(factors):
        value = jnp.full_like(square, factors[-1])
        for factor in factors[-2::-1]:
            value = value * square + factor
        return value

    low_sine = half_angle * series(SINE)
    low_cosine = series(COSINE)
    return 2.0 * low_sine * low_cosine, 1.0 - 2.0 * low_sine * low_sine


def filter_kernel(phase, kernel_cos, kernel_sin, plain):
    rows = lax.broadcasted_iota(jnp.int32, (N, N), 0)
    cols = lax.broadcasted_iota(jnp.int32, (N, N), 1)
    take = (rows == 2 * (cols % HALF) + cols // HALF).astype(F32).astype(BF)
    for col in (0, 1):
        sine, cosine = sine_and_cosine(phase[:, half(col)])
        plain[0, col] = cosine
        plain[1, col] = sine
    for index, out in ((0, kernel_cos), (1, kernel_sin)):
        for parity in (0, 1):
            picked = [plain[index, col, pl.ds(parity, HALF, stride=2), :] for col in (0, 1)]
            rest = jnp.concatenate(picked, 1)
            value = jnp.zeros((HALF, N), F32)
            for _ in range(3):
                term = rest.astype(BF)
                value = value + dot(term, take)
                rest = rest - term.astype(F32)
            out[half(parity), :] = value


def filters(phase):
    shape = jax.ShapeDtypeStruct((N, N), F32)
    return pl.pallas_call(
        filter_kernel,
        name="filters",
        out_shape=[shape, shape],
        scratch_shapes=[pltpu.VMEM((2, 2, N, HALF), F32)],
        compiler_params=pltpu.CompilerParams(vmem_limit_bytes=VMEM_LIMIT),
    )(phase)


def window_kernel(where, offsets, phase_all, amp_all, *rest):
    outs, (field, phase, amp, sems) = rest[:RING], rest[RING:]
    rank = where[0]

    def loads(layer, block):
        rows = half(block)
        return [
            pltpu.make_async_copy(
                source.at[layer, rows, :], target.at[layer, rows, :], sems.at[kind, layer, block]
            )
            for kind, source, target in ((0, phase_all, phase), (1, amp_all, amp))
        ]

    for layer in (0, 1):
        for block in range(3):
            for copy in loads(layer, block):
                copy.start()
    for layer in (0, 1):
        for block in range(3):
            for copy in loads(layer, block):
                copy.wait()
            for col in range(3):
                sine, cosine = sine_and_cosine(phase[layer, half(block), half(col)])
                size = amp[layer, half(block), half(col)]
                field[layer, 0, col, half(block), :] = size * cosine
                field[layer, 1, col, half(block), :] = size * sine
    lane = lax.broadcasted_iota(jnp.int32, (HALF, HALF), 1)
    for distance in range(RING):
        position = (rank + distance) % RING
        col_at = offsets[position, 1]
        turn = (HALF - col_at) % HALF
        inside = lane < HALF - col_at
        for parity in (0, 1):
            rows = pl.ds(offsets[position, 0] + parity, HALF, stride=2)
            for layer in (0, 1):
                for part in (0, 1):
                    turned = [
                        pltpu.roll(field[layer, part, col, rows, :], turn, 1) for col in range(3)
                    ]
                    for col in (0, 1):
                        outs[distance][layer, parity, half(part), half(col)] = jnp.where(
                            inside, turned[col], turned[col + 1]
                        ).astype(BF)


def transmission_windows(where, offsets, phase, amp):
    shape = jax.ShapeDtypeStruct((2, 2, N, N), BF)
    return pl.pallas_call(
        window_kernel,
        name="windows",
        out_shape=[shape] * RING,
        in_specs=[SM, SM, ANY, ANY],
        out_specs=[VM] * RING,
        scratch_shapes=[
            pltpu.VMEM((2, 2, 3, PATCH, HALF), F32),
            pltpu.VMEM((2, PATCH, PATCH), F32),
            pltpu.VMEM((2, PATCH, PATCH), F32),
            pltpu.SemaphoreType.DMA((2, 2, 3)),
        ],
        compiler_params=pltpu.CompilerParams(vmem_limit_bytes=VMEM_LIMIT),
    )(where, offsets, phase, amp)


def chain_kernel(first, where, start, *rest):
    windows = rest[:RING]
    earlier = () if first else rest[RING : 2 * RING]
    rest = rest[RING + len(earlier) :]
    tables = rest[:5]
    count = RING + 1
    outs = rest[5 : 5 + count]
    trans, waves, middle, mixed, filtered, second, in_sems, out_sems = rest[5 + count :]
    rank = where[0]
    active = where[1] == 1 if first else where[1] == 0

    def window_load(distance):
        slot = (rank + RING - distance) % RING
        return pltpu.make_async_copy(windows[distance], trans.at[slot], in_sems.at[slot])

    def store(k):
        return pltpu.make_async_copy(waves.at[k], outs[k], out_sems.at[k])

    @pl.when(active)
    def _():
        begin_load = pltpu.make_async_copy(
            start, waves.at[(2 * RING - 1 - rank) % RING], in_sems.at[RING]
        )
        begin_load.start()
        for distance in range(RING):
            window_load(distance).start()
        begin_load.wait()

        def pair(step, carry):
            pair_at = RING - 1 - step
            slot = (pair_at + RING - rank) % RING
            for k in range(RING):

                @pl.when(slot == k)
                def _(k=k):
                    store(k).start()

            source = waves.at[slot]
            target = waves.at[
                jnp.where(pair_at == 0, RING, (pair_at + 2 * RING - 1 - rank) % RING)
            ]
            for layer, begin, end in ((1, source, middle), (0, middle, target)):

                def ready(layer=layer):
                    if layer == 1:
                        pltpu.make_async_copy(
                            windows[0], trans.at[pair_at], in_sems.at[pair_at]
                        ).wait()

                def finish(parity, reals, imags, layer=layer, end=end):
                    for col in (0, 1):
                        tr = trans[pair_at, layer, parity, half(0), half(col)].astype(F32)
                        ti = trans[pair_at, layer, parity, half(1), half(col)].astype(F32)
                        qr, qi = reals[col], imags[col]
                        end[parity, half(0), half(col)] = (tr * qr + ti * qi).astype(BF)
                        end[parity, half(1), half(col)] = (tr * qi - ti * qr).astype(BF)

                back_step(begin, tables, mixed, filtered, second, finish, ready)
            return carry

        lax.fori_loop(0, RING, pair, 0)
        store(RING).start()
        for k in range(RING + 1):
            store(k).wait()

    if not first:

        @pl.when(jnp.logical_not(active))
        def _():
            copies = [
                pltpu.make_async_copy(earlier[k], outs[k], out_sems.at[k]) for k in range(RING)
            ]
            middle[...] = jnp.zeros_like(middle)
            copies.append(pltpu.make_async_copy(middle, outs[RING], out_sems.at[RING]))
            for copy in copies:
                copy.start()
            for copy in copies:
                copy.wait()


def run_chain(first, where, start, windows, earlier, tables):
    count = RING + 1
    wave = jax.ShapeDtypeStruct((2, N, N), BF)
    return pl.pallas_call(
        functools.partial(chain_kernel, first),
        name="chain_deep" if first else "chain_top",
        out_shape=[wave] * count,
        in_specs=[SM, ANY] + [ANY] * RING + [ANY] * len(earlier) + [VM] * 5,
        out_specs=[ANY] * count,
        scratch_shapes=[
            pltpu.VMEM((RING, 2, 2, N, N), BF),
            pltpu.VMEM((RING + 1, 2, N, N), BF),
            pltpu.VMEM((2, N, N), BF),
            *step_scratch(),
            pltpu.SemaphoreType.DMA((RING + 1,)),
            pltpu.SemaphoreType.DMA((RING + 1,)),
        ],
        compiler_params=pltpu.CompilerParams(vmem_limit_bytes=VMEM_LIMIT),
    )(where, start, *windows, *earlier, *tables)


def visit_kernel(index, where, offsets, entry, window, psi, *rest):
    tables = rest[:5]
    grads, middle, mixed, filtered, second = rest[-5:]
    if index == 0:
        grads[...] = jnp.zeros_like(grads)
    lane = lax.broadcasted_iota(jnp.int32, (HALF, HALF), 1)
    position = (where[0] + RING - index) % RING
    col_at = offsets[position, 1]
    turn = col_at % HALF
    inside = lane >= col_at

    for layer in (1, 0):

        def finish(parity, reals, imags, layer=layer):
            terms = ([], [])
            for col in (0, 1):
                wr = psi[layer, parity, half(0), half(col)].astype(F32)
                wi = psi[layer, parity, half(1), half(col)].astype(F32)
                qr, qi = reals[col], imags[col]
                terms[0].append(pltpu.roll(wr * qr + wi * qi, turn, 1))
                terms[1].append(pltpu.roll(wr * qi - wi * qr, turn, 1))
                if layer == 1:
                    tr = window[layer, parity, half(0), half(col)].astype(F32)
                    ti = window[layer, parity, half(1), half(col)].astype(F32)
                    middle[parity, half(0), half(col)] = (tr * qr + ti * qi).astype(BF)
                    middle[parity, half(1), half(col)] = (tr * qi - ti * qr).astype(BF)
            rows = pl.ds(offsets[position, 0] + parity, HALF, stride=2)
            zero = jnp.zeros((HALF, HALF), F32)
            for part in (0, 1):
                left, right = terms[part]
                placed = (
                    jnp.where(inside, left, zero),
                    jnp.where(inside, right, left),
                    jnp.where(inside, zero, right),
                )
                for col in range(3):
                    grads[layer, part, col, rows, :] += placed[col]

        back_step(entry if layer == 1 else middle, tables, mixed, filtered, second, finish)


def visit(index, where, offsets, entry, window, psi, tables, grads):
    earlier = () if index == 0 else (grads,)
    return pl.pallas_call(
        functools.partial(visit_kernel, index),
        name=f"visit_{index}",
        out_shape=jax.ShapeDtypeStruct((2, 2, 3, PATCH, HALF), F32),
        in_specs=[SM, SM] + [VM] * (8 + len(earlier)),
        out_specs=VM,
        scratch_shapes=[pltpu.VMEM((2, N, N), BF), *step_scratch()],
        input_output_aliases={10: 0} if earlier else {},
        compiler_params=pltpu.CompilerParams(vmem_limit_bytes=VMEM_LIMIT),
    )(where, offsets, entry, window, psi, *tables, *earlier)


def pack_kernel(grads, probe, payload, summed):
    chunks = payload.shape[0]
    rows_each = PATCH // chunks
    total = jnp.zeros((HALF, HALF), F32)
    for source in range(DEPTH):
        total = total + probe[source].astype(F32)
    summed[...] = total
    for chunk in range(chunks):
        rows = slice(chunk * rows_each, (chunk + 1) * rows_each)
        for col in range(3):
            pieces = [grads[layer, part, col, rows, :] for layer in (0, 1) for part in (0, 1)]
            own = slice(8 * chunk, 8 * chunk + 8)
            pieces.append(summed[own, :] if col == 0 else jnp.zeros((8, HALF), F32))
            pieces.append(jnp.zeros((8, HALF), F32))
            payload[chunk, :, half(col)] = jnp.concatenate(pieces, 0).astype(BF)


def packed(chunks, grads, probe):
    rows = 4 * (PATCH // chunks) + 16
    return pl.pallas_call(
        pack_kernel,
        name="pack",
        out_shape=jax.ShapeDtypeStruct((chunks, rows, PATCH), BF),
        in_specs=[VM, VM],
        out_specs=VM,
        scratch_shapes=[pltpu.VMEM((HALF, HALF), F32)],
        compiler_params=pltpu.CompilerParams(vmem_limit_bytes=VMEM_LIMIT),
    )(grads, probe)


def order_kernel(where, residual, saved, start, *rest):
    outs, (first, waves, sems) = rest[:RING], rest[RING:]
    rank = where[0]
    loads = [pltpu.make_async_copy(residual.at[rank], first, sems.at[RING])]
    for index in range(RING):
        position = (rank + RING - index) % RING
        loads.append(
            pltpu.make_async_copy(saved.at[:, position], waves.at[index], sems.at[index])
        )
    for copy in loads:
        copy.start()
    rows = lax.broadcasted_iota(jnp.int32, (N, N), 0)
    cols = lax.broadcasted_iota(jnp.int32, (N, N), 1)
    take = (cols == 2 * (rows % HALF) + rows // HALF).astype(F32).astype(BF)

    def reorder(source, target):
        for part in (0, 1):
            ordered = dot(take, source[part]).astype(BF)
            for parity in (0, 1):
                target[parity, half(part), :] = ordered[half(parity), :]

    loads[0].wait()
    reorder(first, start)
    for index in range(RING):
        loads[1 + index].wait()
        for layer in (0, 1):
            reorder(waves.at[index, layer], outs[index].at[layer])


def row_parity_first(where, residual, saved):
    wave = (2, N, N)
    return pl.pallas_call(
        order_kernel,
        name="reorder",
        out_shape=[jax.ShapeDtypeStruct(wave, BF)]
        + [jax.ShapeDtypeStruct((2, *wave), BF)] * RING,
        in_specs=[SM, ANY, ANY],
        out_specs=[VM] * (RING + 1),
        scratch_shapes=[
            pltpu.VMEM(wave, BF),
            pltpu.VMEM((RING, 2, *wave), BF),
            pltpu.SemaphoreType.DMA((RING + 1,)),
        ],
        compiler_params=pltpu.CompilerParams(vmem_limit_bytes=VMEM_LIMIT),
    )(where, residual, saved)


def pieces_kernel(wave, pieces):
    width = N // DEPTH
    lane = lax.broadcasted_iota(jnp.int32, (HALF, HALF), 1) // width
    for piece in range(DEPTH):
        per_tile = HALF // width
        value = jnp.zeros((HALF, HALF), F32)
        for parity in (0, 1):
            for part in (0, 1):
                place = 2 * parity + part
                source = wave[parity, half(part), half(piece // per_tile)].astype(F32)
                shift = (place - piece % per_tile) * width % HALF
                moved = pltpu.roll(source, shift, 1) if shift else source
                value = jnp.where(lane == place, moved, value)
        pieces[piece] = value.astype(BF)


def column_pieces(wave):
    return pl.pallas_call(
        pieces_kernel,
        name="pieces",
        out_shape=jax.ShapeDtypeStruct((DEPTH, HALF, HALF), BF),
        compiler_params=pltpu.CompilerParams(vmem_limit_bytes=VMEM_LIMIT),
    )(wave)


def total_kernel(received, rows_out, probe_out):
    chunks, rows, _ = received.shape
    whole = rows - 16
    for at in range(0, rows, 16):
        value = received[0, at : at + 16, :].astype(F32)
        for chunk in range(1, chunks):
            value = value + received[chunk, at : at + 16, :].astype(F32)
        if at < whole:
            rows_out[at : at + 16, :] = value
        else:
            probe_out[...] = value[:8, :HALF]


def totals(received):
    _, rows, _ = received.shape
    return pl.pallas_call(
        total_kernel,
        name="totals",
        out_shape=[
            jax.ShapeDtypeStruct((rows - 16, PATCH), F32),
            jax.ShapeDtypeStruct((8, HALF), F32),
        ],
        compiler_params=pltpu.CompilerParams(vmem_limit_bytes=VMEM_LIMIT),
    )(received)


def turned(array, distance):
    route = [
        (RING * ring + i, RING * ring + (i + distance) % RING)
        for ring in range(2)
        for i in range(RING)
    ]
    return lax.ppermute(array, "depth", route)


def exchanged(arrays):
    return [arrays[0]] + [turned(arrays[k], k) for k in range(1, RING)]


def shards(residual, saved_waves, object_phase, object_amp, prop_phase, offsets):
    depth_at = lax.axis_index("depth")
    chunks = lax.axis_size("probe")
    where = jnp.stack([depth_at % RING, depth_at // RING]).astype(jnp.int32)
    own = transmission_windows(where, offsets, object_phase, object_amp)
    tables = (*transform_tables(N), *filters(prop_phase))
    start, *waves = row_parity_first(where, residual, saved_waves)
    foreign = exchanged(own)
    *deep, leaving = run_chain(True, where, start, foreign, (), tables)
    arrived = lax.ppermute(leaving, "depth", [(RING + i, i) for i in range(RING)])
    *entries, ending = run_chain(False, where, arrived, foreign, deep, tables)
    entries = exchanged(entries)
    probe = lax.all_to_all(column_pieces(ending), "depth", 0, 0, tiled=True)
    grads = None
    for index in (0, 3, 1, 2):
        window = own[(RING - index) % RING]
        grads = visit(
            index, where, offsets, entries[index], window, waves[index], tables, grads
        )
    payload = packed(chunks, grads, probe)
    received = lax.all_to_all(payload, "probe", 0, 0, tiled=True)
    rows, probe_rows = totals(received)
    object_grad = rows.reshape(2, 2, PATCH // chunks, PATCH)
    probe_grad = probe_rows.reshape(8, 2, 2, N // DEPTH).transpose(2, 0, 1, 3)
    return (object_grad, probe_grad.reshape(2, 16, N // DEPTH))


def solution(mesh):
    return jax.shard_map(
        shards,
        mesh=mesh,
        in_specs=(
            P("probe", None, None, None),
            P("depth", "probe", None, None, None),
            P("depth", None, None),
            P("depth", None, None),
            P(),
            P("probe", None),
        ),
        out_specs=(P("depth", None, "probe", None), P(None, "probe", "depth")),
        check_vma=False,
    )
```

```python
import functools
import math

import jax
import jax.numpy as jnp
from jax import lax
from jax.experimental import pallas as pl
from jax.experimental.pallas import tpu as pltpu
from jax.sharding import PartitionSpec as P

BF = jnp.bfloat16
F32 = jnp.float32
RING = 4
FAR = 2
DEPTH = 8
N = 256
HALF = 128
PATCH = 384
ANY = pl.BlockSpec(memory_space=pl.ANY)
VM = pl.BlockSpec(memory_space=pltpu.VMEM)
SM = pl.BlockSpec(memory_space=pltpu.SMEM)
SINE = (0.999999995716, -0.166666579699, 0.00833305061733, -0.000198090463574, 2.60516627618e-06)
COSINE = (0.99999999978, -0.49999999357, 0.0416666362089, -0.00138883608423, 2.47601355058e-05, -2.60510761786e-07)
VMEM_LIMIT = 20 * 1024 * 1024


def in_hbm(array):
    return pltpu.with_memory_space_constraint(array, pltpu.HBM)


def half(index):
    return slice(index * HALF, (index + 1) * HALF)


def transform_tables(width):
    span = width // 2
    shape = (2, width, width)
    parity = lax.broadcasted_iota(jnp.int32, shape, 0)

    def build(spread_dim, sign):
        rows = lax.broadcasted_iota(jnp.int32, shape, 1)
        cols = lax.broadcasted_iota(jnp.int32, shape, 2)
        spread, other = (rows, cols) if spread_dim == 1 else (cols, rows)
        order = (2 * (spread % span) + parity) * (other % span) % width
        phase = 2.0 * math.pi / width * order.astype(F32)
        factor = 1.0 / math.sqrt(width)
        low = rows < span
        left = cols < span
        value = jnp.where(low == left, jnp.cos(phase), jnp.where(low, sign, -sign) * jnp.sin(phase))
        return (value * factor).astype(BF)

    return build(2, 1.0), build(1, 1.0), build(2, -1.0)


def dot(a, b):
    return jnp.dot(a, b, preferred_element_type=F32)


def back_step(source, tables, mixed, filtered, second, finish, ready=None):
    inward, table, flipped, kernel_cos, kernel_sin = tables
    for part in (0, 1):
        even = dot(inward[0, half(part), :], source[0])
        odd = dot(inward[1, half(part), :], source[1])
        for row, value in ((0, even + odd), (1, even - odd)):
            left, right = value[:, :HALF], value[:, HALF:]
            mixed[0, half(row), half(part)] = (left + right).astype(BF)
            mixed[1, half(row), half(part)] = (left - right).astype(BF)
    for col in (0, 1):
        upper = dot(mixed[col, half(0), :], flipped[col])
        lower = dot(mixed[col, half(1), :], flipped[col])
        for parity in (0, 1):
            real = upper[:, half(parity)]
            imag = lower[:, half(parity)]
            kc = kernel_cos[half(parity), half(col)]
            ks = kernel_sin[half(parity), half(col)]
            filtered[parity, half(0), half(col)] = (kc * real + ks * imag).astype(BF)
            filtered[parity, half(1), half(col)] = (kc * imag - ks * real).astype(BF)
    for part in (0, 1):
        even = dot(flipped[0, half(part), :], filtered[0])
        odd = dot(flipped[1, half(part), :], filtered[1])
        total = (even + odd).astype(BF)
        diff = (even - odd).astype(BF)
        for col in (0, 1):
            second[col, half(0), half(part)] = total[:, half(col)]
            second[col, half(1), half(part)] = diff[:, half(col)]
    if ready is not None:
        ready()
    totals, diffs = [], []
    for row in (0, 1):
        even = dot(second[0, half(row), :], table[0])
        odd = dot(second[1, half(row), :], table[1])
        totals.append(even + odd)
        diffs.append(even - odd)
    for parity in (0, 1):
        finish(
            parity,
            (totals[0][:, half(parity)], diffs[0][:, half(parity)]),
            (totals[1][:, half(parity)], diffs[1][:, half(parity)]),
        )


def step_scratch():
    return [pltpu.VMEM((2, N, N), BF), pltpu.VMEM((2, N, N), BF), pltpu.VMEM((2, N, N), BF)]


def sine_and_cosine(angle):
    half_angle = 0.5 * angle
    square = half_angle * half_angle

    def series(factors):
        value = jnp.full_like(square, factors[-1])
        for factor in factors[-2::-1]:
            value = value * square + factor
        return value

    low_sine = half_angle * series(SINE)
    low_cosine = series(COSINE)
    return 2.0 * low_sine * low_cosine, 1.0 - 2.0 * low_sine * low_sine


def filter_kernel(phase, kernel_cos, kernel_sin, plain):
    rows = lax.broadcasted_iota(jnp.int32, (N, N), 0)
    cols = lax.broadcasted_iota(jnp.int32, (N, N), 1)
    take = (rows == 2 * (cols % HALF) + cols // HALF).astype(F32).astype(BF)
    for col in (0, 1):
        sine, cosine = sine_and_cosine(phase[:, half(col)])
        plain[0, col] = cosine
        plain[1, col] = sine
    for index, out in ((0, kernel_cos), (1, kernel_sin)):
        for parity in (0, 1):
            picked = [plain[index, col, pl.ds(parity, HALF, stride=2), :] for col in (0, 1)]
            rest = jnp.concatenate(picked, 1)
            value = jnp.zeros((HALF, N), F32)
            for _ in range(3):
                term = rest.astype(BF)
                value = value + dot(term, take)
                rest = rest - term.astype(F32)
            out[half(parity), :] = value


def filters(phase):
    shape = jax.ShapeDtypeStruct((N, N), F32)
    return pl.pallas_call(
        filter_kernel,
        name="filters",
        out_shape=[shape, shape],
        scratch_shapes=[pltpu.VMEM((2, 2, N, HALF), F32)],
        compiler_params=pltpu.CompilerParams(vmem_limit_bytes=VMEM_LIMIT),
    )(phase)


def window_kernel(where, offsets, phase_all, amp_all, *rest):
    outs, (field, phase, amp, sems) = rest[: RING + 1], rest[RING + 1 :]
    rank = where[0]

    def loads(layer, block):
        rows = half(block)
        return [
            pltpu.make_async_copy(
                source.at[layer, rows, :], target.at[layer, rows, :], sems.at[kind, layer, block]
            )
            for kind, source, target in ((0, phase_all, phase), (1, amp_all, amp))
        ]

    for layer in (0, 1):
        for block in range(3):
            for copy in loads(layer, block):
                copy.start()
    for layer in (0, 1):
        for block in range(3):
            for copy in loads(layer, block):
                copy.wait()
            for col in range(3):
                sine, cosine = sine_and_cosine(phase[layer, half(block), half(col)])
                size = amp[layer, half(block), half(col)]
                field[layer, 0, col, half(block), :] = size * cosine
                field[layer, 1, col, half(block), :] = size * sine
    lane = lax.broadcasted_iota(jnp.int32, (HALF, HALF), 1)
    for distance in range(RING):
        position = (rank + distance) % RING
        col_at = offsets[position, 1]
        turn = (HALF - col_at) % HALF
        inside = lane < HALF - col_at
        for parity in (0, 1):
            rows = pl.ds(offsets[position, 0] + parity, HALF, stride=2)
            for layer in (0, 1):
                for part in (0, 1):
                    turned = [
                        pltpu.roll(field[layer, part, col, rows, :], turn, 1) for col in range(3)
                    ]
                    if distance == FAR:
                        target = outs[distance if layer else RING]
                    else:
                        target = outs[distance].at[layer]
                    for col in (0, 1):
                        target[parity, half(part), half(col)] = jnp.where(
                            inside, turned[col], turned[col + 1]
                        ).astype(BF)


def transmission_windows(where, offsets, phase, amp):
    both = jax.ShapeDtypeStruct((2, 2, N, N), BF)
    single = jax.ShapeDtypeStruct((2, N, N), BF)
    return pl.pallas_call(
        window_kernel,
        name="windows",
        out_shape=[both, both, single, both, single],
        in_specs=[SM, SM, ANY, ANY],
        out_specs=[VM] * (RING + 1),
        scratch_shapes=[
            pltpu.VMEM((2, 2, 3, PATCH, HALF), F32),
            pltpu.VMEM((2, PATCH, PATCH), F32),
            pltpu.VMEM((2, PATCH, PATCH), F32),
            pltpu.SemaphoreType.DMA((2, 2, 3)),
        ],
        compiler_params=pltpu.CompilerParams(vmem_limit_bytes=VMEM_LIMIT),
    )(where, offsets, in_hbm(phase), in_hbm(amp))


def chain_kernel(first, where, start, *rest):
    windows = rest[: RING + 1]
    earlier = () if first else rest[RING + 1 : 2 * RING + 1]
    rest = rest[RING + 1 + len(earlier) :]
    tables = rest[:5]
    count = RING + 1
    outs = rest[5 : 5 + count]
    trans, waves, middle, mixed, filtered, second, in_sems, out_sems = rest[5 + count :]
    rank = where[0]
    active = where[1] == 1 if first else where[1] == 0

    def window_load(distance, layer):
        slot = (rank + RING - distance) % RING
        if distance == FAR:
            source = windows[distance if layer else RING]
        else:
            source = windows[distance].at[layer]
        return pltpu.make_async_copy(source, trans.at[slot, layer], in_sems.at[slot, layer])

    def store(k):
        return pltpu.make_async_copy(waves.at[k], outs[k], out_sems.at[k])

    @pl.when(active)
    def _():
        begin_load = pltpu.make_async_copy(
            start, waves.at[(2 * RING - 1 - rank) % RING], in_sems.at[RING, 0]
        )
        begin_load.start()
        for distance in range(RING):
            for layer in (1, 0):
                window_load(distance, layer).start()
        begin_load.wait()

        def pair(step, carry):
            pair_at = RING - 1 - step
            slot = (pair_at + RING - rank) % RING
            for k in range(RING):

                @pl.when(slot == k)
                def _(k=k):
                    store(k).start()

            source = waves.at[slot]
            target = waves.at[
                jnp.where(pair_at == 0, RING, (pair_at + 2 * RING - 1 - rank) % RING)
            ]
            for layer, begin, end in ((1, source, middle), (0, middle, target)):

                def ready(layer=layer):
                    pltpu.make_async_copy(
                        windows[0].at[layer], trans.at[pair_at, layer], in_sems.at[pair_at, layer]
                    ).wait()

                def finish(parity, reals, imags, layer=layer, end=end):
                    for col in (0, 1):
                        tr = trans[pair_at, layer, parity, half(0), half(col)].astype(F32)
                        ti = trans[pair_at, layer, parity, half(1), half(col)].astype(F32)
                        qr, qi = reals[col], imags[col]
                        end[parity, half(0), half(col)] = (tr * qr + ti * qi).astype(BF)
                        end[parity, half(1), half(col)] = (tr * qi - ti * qr).astype(BF)

                back_step(begin, tables, mixed, filtered, second, finish, ready)
            return carry

        lax.fori_loop(0, RING, pair, 0)
        store(RING).start()
        for k in range(RING + 1):
            store(k).wait()

    if not first:

        @pl.when(jnp.logical_not(active))
        def _():
            copies = [
                pltpu.make_async_copy(earlier[k], outs[k], out_sems.at[k]) for k in range(RING)
            ]
            middle[...] = jnp.zeros_like(middle)
            copies.append(pltpu.make_async_copy(middle, outs[RING], out_sems.at[RING]))
            for copy in copies:
                copy.start()
            for copy in copies:
                copy.wait()


def run_chain(first, where, start, windows, earlier, tables):
    count = RING + 1
    wave = jax.ShapeDtypeStruct((2, N, N), BF)
    return pl.pallas_call(
        functools.partial(chain_kernel, first),
        name="chain_deep" if first else "chain_top",
        out_shape=[wave] * count,
        in_specs=[SM, ANY] + [ANY] * (RING + 1) + [ANY] * len(earlier) + [VM] * 5,
        out_specs=[ANY] * count,
        scratch_shapes=[
            pltpu.VMEM((RING, 2, 2, N, N), BF),
            pltpu.VMEM((RING + 1, 2, N, N), BF),
            pltpu.VMEM((2, N, N), BF),
            *step_scratch(),
            pltpu.SemaphoreType.DMA((RING + 1, 2)),
            pltpu.SemaphoreType.DMA((RING + 1,)),
        ],
        compiler_params=pltpu.CompilerParams(vmem_limit_bytes=VMEM_LIMIT),
    )(where, start, *windows, *earlier, *tables)


def visit_kernel(index, where, offsets, entry_at, window_at, psi_at, *rest):
    tables = rest[:5]
    grads, entry, window, psi, middle, mixed, filtered, second, sems = rest[-9:]
    loads = [
        pltpu.make_async_copy(entry_at, entry, sems.at[0]),
        pltpu.make_async_copy(window_at if index == FAR else window_at.at[1], window, sems.at[1]),
        pltpu.make_async_copy(psi_at, psi, sems.at[2]),
    ]
    for copy in loads:
        copy.start()
    if index == 0:
        grads[...] = jnp.zeros_like(grads)
    lane = lax.broadcasted_iota(jnp.int32, (HALF, HALF), 1)
    position = (where[0] + RING - index) % RING
    col_at = offsets[position, 1]
    turn = col_at % HALF
    inside = lane >= col_at
    loads[0].wait()

    def ready():
        loads[1].wait()
        loads[2].wait()

    for layer in (1, 0):

        def finish(parity, reals, imags, layer=layer):
            terms = ([], [])
            for col in (0, 1):
                wr = psi[layer, parity, half(0), half(col)].astype(F32)
                wi = psi[layer, parity, half(1), half(col)].astype(F32)
                qr, qi = reals[col], imags[col]
                terms[0].append(pltpu.roll(wr * qr + wi * qi, turn, 1))
                terms[1].append(pltpu.roll(wr * qi - wi * qr, turn, 1))
                if layer == 1:
                    tr = window[parity, half(0), half(col)].astype(F32)
                    ti = window[parity, half(1), half(col)].astype(F32)
                    middle[parity, half(0), half(col)] = (tr * qr + ti * qi).astype(BF)
                    middle[parity, half(1), half(col)] = (tr * qi - ti * qr).astype(BF)
            rows = pl.ds(offsets[position, 0] + parity, HALF, stride=2)
            zero = jnp.zeros((HALF, HALF), F32)
            for part in (0, 1):
                left, right = terms[part]
                placed = (
                    jnp.where(inside, left, zero),
                    jnp.where(inside, right, left),
                    jnp.where(inside, zero, right),
                )
                for col in range(3):
                    grads[layer, part, col, rows, :] += placed[col]

        if layer == 1:
            back_step(entry, tables, mixed, filtered, second, finish, ready)
        else:
            back_step(middle, tables, mixed, filtered, second, finish)


def visit(index, where, offsets, entry, window, psi, tables, grads):
    earlier = () if index == 0 else (grads,)
    return pl.pallas_call(
        functools.partial(visit_kernel, index),
        name=f"visit_{index}",
        out_shape=jax.ShapeDtypeStruct((2, 2, 3, PATCH, HALF), F32),
        in_specs=[SM, SM] + [ANY] * 3 + [VM] * (5 + len(earlier)),
        out_specs=VM,
        scratch_shapes=[
            pltpu.VMEM((2, N, N), BF),
            pltpu.VMEM((2, N, N), BF),
            pltpu.VMEM((2, 2, N, N), BF),
            pltpu.VMEM((2, N, N), BF),
            *step_scratch(),
            pltpu.SemaphoreType.DMA((3,)),
        ],
        input_output_aliases={10: 0} if earlier else {},
        compiler_params=pltpu.CompilerParams(vmem_limit_bytes=VMEM_LIMIT),
    )(where, offsets, *(in_hbm(array) for array in (entry, window, psi)), *tables, *earlier)


def pack_kernel(grads, probe, payload, summed):
    chunks = payload.shape[0]
    rows_each = PATCH // chunks
    total = jnp.zeros((HALF, HALF), F32)
    for source in range(DEPTH):
        total = total + probe[source].astype(F32)
    summed[...] = total
    for chunk in range(chunks):
        rows = slice(chunk * rows_each, (chunk + 1) * rows_each)
        for col in range(3):
            pieces = [grads[layer, part, col, rows, :] for layer in (0, 1) for part in (0, 1)]
            own = slice(8 * chunk, 8 * chunk + 8)
            pieces.append(summed[own, :] if col == 0 else jnp.zeros((8, HALF), F32))
            pieces.append(jnp.zeros((8, HALF), F32))
            payload[chunk, :, half(col)] = jnp.concatenate(pieces, 0).astype(BF)


def packed(chunks, grads, probe):
    rows = 4 * (PATCH // chunks) + 16
    return pl.pallas_call(
        pack_kernel,
        name="pack",
        out_shape=jax.ShapeDtypeStruct((chunks, rows, PATCH), BF),
        in_specs=[VM, VM],
        out_specs=VM,
        scratch_shapes=[pltpu.VMEM((HALF, HALF), F32)],
        compiler_params=pltpu.CompilerParams(vmem_limit_bytes=VMEM_LIMIT),
    )(grads, probe)


def order_kernel(where, residual, saved, start, *rest):
    outs, (first, waves, done, sems, out_sems) = rest[:RING], rest[RING:]
    rank = where[0]
    loads = [pltpu.make_async_copy(residual.at[rank], first, sems.at[RING])]
    for index in range(RING):
        position = (rank + RING - index) % RING
        loads.append(
            pltpu.make_async_copy(saved.at[:, position], waves.at[index], sems.at[index])
        )
    for copy in loads:
        copy.start()
    rows = lax.broadcasted_iota(jnp.int32, (N, N), 0)
    cols = lax.broadcasted_iota(jnp.int32, (N, N), 1)
    take = (cols == 2 * (rows % HALF) + rows // HALF).astype(F32).astype(BF)

    def reorder(source, target):
        for part in (0, 1):
            ordered = dot(take, source[part]).astype(BF)
            for parity in (0, 1):
                target[parity, half(part), :] = ordered[half(parity), :]

    stores = []
    loads[0].wait()
    reorder(first, start)
    for index in range(RING):
        loads[1 + index].wait()
        for layer in (0, 1):
            reorder(waves.at[index, layer], done.at[index, layer])
        stores.append(pltpu.make_async_copy(done.at[index], outs[index], out_sems.at[index]))
        stores[-1].start()
    for copy in stores:
        copy.wait()


def row_parity_first(where, residual, saved):
    wave = (2, N, N)
    return pl.pallas_call(
        order_kernel,
        name="reorder",
        out_shape=[jax.ShapeDtypeStruct(wave, BF)]
        + [jax.ShapeDtypeStruct((2, *wave), BF)] * RING,
        in_specs=[SM, ANY, ANY],
        out_specs=[VM] + [pl.BlockSpec(memory_space=pltpu.HBM)] * RING,
        scratch_shapes=[
            pltpu.VMEM(wave, BF),
            pltpu.VMEM((RING, 2, *wave), BF),
            pltpu.VMEM((RING, 2, *wave), BF),
            pltpu.SemaphoreType.DMA((RING + 1,)),
            pltpu.SemaphoreType.DMA((RING,)),
        ],
        compiler_params=pltpu.CompilerParams(vmem_limit_bytes=VMEM_LIMIT),
    )(where, in_hbm(residual), in_hbm(saved))


def pieces_kernel(wave, pieces):
    width = N // DEPTH
    lane = lax.broadcasted_iota(jnp.int32, (HALF, HALF), 1) // width
    for piece in range(DEPTH):
        per_tile = HALF // width
        value = jnp.zeros((HALF, HALF), F32)
        for parity in (0, 1):
            for part in (0, 1):
                place = 2 * parity + part
                source = wave[parity, half(part), half(piece // per_tile)].astype(F32)
                shift = (place - piece % per_tile) * width % HALF
                moved = pltpu.roll(source, shift, 1) if shift else source
                value = jnp.where(lane == place, moved, value)
        pieces[piece] = value.astype(BF)


def column_pieces(wave):
    return pl.pallas_call(
        pieces_kernel,
        name="pieces",
        out_shape=jax.ShapeDtypeStruct((DEPTH, HALF, HALF), BF),
        compiler_params=pltpu.CompilerParams(vmem_limit_bytes=VMEM_LIMIT),
    )(wave)


def total_kernel(received, rows_out, probe_out):
    chunks, rows, _ = received.shape
    whole = rows - 16
    for at in range(0, rows, 16):
        value = received[0, at : at + 16, :].astype(F32)
        for chunk in range(1, chunks):
            value = value + received[chunk, at : at + 16, :].astype(F32)
        if at < whole:
            rows_out[at : at + 16, :] = value
        else:
            probe_out[...] = value[:8, :HALF]


def totals(received):
    _, rows, _ = received.shape
    return pl.pallas_call(
        total_kernel,
        name="totals",
        out_shape=[
            jax.ShapeDtypeStruct((rows - 16, PATCH), F32),
            jax.ShapeDtypeStruct((8, HALF), F32),
        ],
        compiler_params=pltpu.CompilerParams(vmem_limit_bytes=VMEM_LIMIT),
    )(received)


def turned(array, distance):
    route = [
        (RING * ring + i, RING * ring + (i + distance) % RING)
        for ring in range(2)
        for i in range(RING)
    ]
    return lax.ppermute(array, "depth", route)


def exchanged(arrays):
    return [arrays[0]] + [turned(arrays[k], k) for k in range(1, RING)]


def exchanged_windows(own):
    relay = turned(own[RING], RING - 1)
    back = turned(own[3], 3)
    far = turned(own[FAR], FAR)
    ahead = turned(own[1], 1)
    return [own[0], ahead, far, back, turned(relay, RING - 1)]


def shards(residual, saved_waves, object_phase, object_amp, prop_phase, offsets):
    depth_at = lax.axis_index("depth")
    chunks = lax.axis_size("probe")
    where = jnp.stack([depth_at % RING, depth_at // RING]).astype(jnp.int32)
    own = transmission_windows(where, offsets, object_phase, object_amp)
    tables = (*transform_tables(N), *filters(prop_phase))
    start, *waves = row_parity_first(where, residual, saved_waves)
    foreign = exchanged_windows(own)
    *deep, leaving = run_chain(True, where, start, foreign, (), tables)
    arrived = lax.ppermute(leaving, "depth", [(RING + i, i) for i in range(RING)])
    *entries, ending = run_chain(False, where, arrived, foreign, deep, tables)
    entries = exchanged(entries)
    grads = None
    for index in (0, 3, 1, 2):
        window = own[(RING - index) % RING]
        grads = visit(
            index, where, offsets, entries[index], window, waves[index], tables, grads
        )
        if index == 0:
            ending, grads = lax.optimization_barrier((ending, grads))
            probe = lax.all_to_all(column_pieces(ending), "depth", 0, 0, tiled=True)
    payload = packed(chunks, grads, probe)
    received = lax.all_to_all(payload, "probe", 0, 0, tiled=True)
    rows, probe_rows = totals(received)
    object_grad = rows.reshape(2, 2, PATCH // chunks, PATCH)
    probe_grad = probe_rows.reshape(8, 2, 2, N // DEPTH).transpose(2, 0, 1, 3)
    return (object_grad, probe_grad.reshape(2, 16, N // DEPTH))


def solution(mesh):
    return jax.shard_map(
        shards,
        mesh=mesh,
        in_specs=(
            P("probe", None, None, None),
            P("depth", "probe", None, None, None),
            P("depth", None, None),
            P("depth", None, None),
            P(),
            P("probe", None),
        ),
        out_specs=(P("depth", None, "probe", None), P(None, "probe", "depth")),
        check_vma=False,
    )
```

```python
import functools
import math

import jax
import jax.numpy as jnp
from jax import lax
from jax.experimental import pallas as pl
from jax.experimental.pallas import tpu as pltpu
from jax.sharding import PartitionSpec as P

BF = jnp.bfloat16
F32 = jnp.float32
RING = 4
DEPTH = 8
N = 256
HALF = 128
PATCH = 384
EACH = PATCH // 16
CHUNK = 4 * EACH + 16
ANY = pl.BlockSpec(memory_space=pl.ANY)
VM = pl.BlockSpec(memory_space=pltpu.VMEM)
SM = pl.BlockSpec(memory_space=pltpu.SMEM)
SINE = (0.999999995716, -0.166666579699, 0.00833305061733, -0.000198090463574, 2.60516627618e-06)
COSINE = (0.99999999978, -0.49999999357, 0.0416666362089, -0.00138883608423, 2.47601355058e-05, -2.60510761786e-07)
VMEM_LIMIT = 20 * 1024 * 1024


def in_hbm(array):
    return pltpu.with_memory_space_constraint(array, pltpu.HBM)


def half(index):
    return slice(index * HALF, (index + 1) * HALF)


def transform_tables(width):
    span = width // 2
    shape = (2, width, width)
    parity = lax.broadcasted_iota(jnp.int32, shape, 0)

    def build(spread_dim, sign):
        rows = lax.broadcasted_iota(jnp.int32, shape, 1)
        cols = lax.broadcasted_iota(jnp.int32, shape, 2)
        spread, other = (rows, cols) if spread_dim == 1 else (cols, rows)
        order = (2 * (spread % span) + parity) * (other % span) % width
        phase = 2.0 * math.pi / width * order.astype(F32)
        factor = 1.0 / math.sqrt(width)
        low = rows < span
        left = cols < span
        value = jnp.where(low == left, jnp.cos(phase), jnp.where(low, sign, -sign) * jnp.sin(phase))
        return (value * factor).astype(BF)

    return build(2, 1.0), build(1, 1.0), build(2, -1.0)


def dot(a, b):
    return jnp.dot(a, b, preferred_element_type=F32)


def back_step(source, tables, mixed, filtered, second, finish, ready=None):
    inward, table, flipped, kernel_cos, kernel_sin = tables
    for part in (0, 1):
        even = dot(inward[0, half(part), :], source[0])
        odd = dot(inward[1, half(part), :], source[1])
        for row, value in ((0, even + odd), (1, even - odd)):
            left, right = value[:, :HALF], value[:, HALF:]
            mixed[0, half(row), half(part)] = (left + right).astype(BF)
            mixed[1, half(row), half(part)] = (left - right).astype(BF)
    for col in (0, 1):
        upper = dot(mixed[col, half(0), :], flipped[col])
        lower = dot(mixed[col, half(1), :], flipped[col])
        for parity in (0, 1):
            real = upper[:, half(parity)]
            imag = lower[:, half(parity)]
            kc = kernel_cos[half(parity), half(col)]
            ks = kernel_sin[half(parity), half(col)]
            filtered[parity, half(0), half(col)] = (kc * real + ks * imag).astype(BF)
            filtered[parity, half(1), half(col)] = (kc * imag - ks * real).astype(BF)
    for part in (0, 1):
        even = dot(flipped[0, half(part), :], filtered[0])
        odd = dot(flipped[1, half(part), :], filtered[1])
        total = (even + odd).astype(BF)
        diff = (even - odd).astype(BF)
        for col in (0, 1):
            second[col, half(0), half(part)] = total[:, half(col)]
            second[col, half(1), half(part)] = diff[:, half(col)]
    if ready is not None:
        ready()
    totals, diffs = [], []
    for row in (0, 1):
        even = dot(second[0, half(row), :], table[0])
        odd = dot(second[1, half(row), :], table[1])
        totals.append(even + odd)
        diffs.append(even - odd)
    for parity in (0, 1):
        finish(
            parity,
            (totals[0][:, half(parity)], diffs[0][:, half(parity)]),
            (totals[1][:, half(parity)], diffs[1][:, half(parity)]),
        )


def step_scratch():
    return [pltpu.VMEM((2, N, N), BF), pltpu.VMEM((2, N, N), BF), pltpu.VMEM((2, N, N), BF)]


def sine_and_cosine(angle):
    half_angle = 0.5 * angle
    square = half_angle * half_angle

    def series(factors):
        value = jnp.full_like(square, factors[-1])
        for factor in factors[-2::-1]:
            value = value * square + factor
        return value

    low_sine = half_angle * series(SINE)
    low_cosine = series(COSINE)
    return 2.0 * low_sine * low_cosine, 1.0 - 2.0 * low_sine * low_sine


def filter_kernel(phase, kernel_cos, kernel_sin, plain):
    rows = lax.broadcasted_iota(jnp.int32, (N, N), 0)
    cols = lax.broadcasted_iota(jnp.int32, (N, N), 1)
    take = (rows == 2 * (cols % HALF) + cols // HALF).astype(F32).astype(BF)
    for col in (0, 1):
        sine, cosine = sine_and_cosine(phase[:, half(col)])
        plain[0, col] = cosine
        plain[1, col] = sine
    for index, out in ((0, kernel_cos), (1, kernel_sin)):
        for parity in (0, 1):
            picked = [plain[index, col, pl.ds(parity, HALF, stride=2), :] for col in (0, 1)]
            rest = jnp.concatenate(picked, 1)
            value = jnp.zeros((HALF, N), F32)
            for _ in range(3):
                term = rest.astype(BF)
                value = value + dot(term, take)
                rest = rest - term.astype(F32)
            out[half(parity), :] = value


def filters(phase):
    shape = jax.ShapeDtypeStruct((N, N), F32)
    return pl.pallas_call(
        filter_kernel,
        name="filters",
        out_shape=[shape, shape],
        scratch_shapes=[pltpu.VMEM((2, 2, N, HALF), F32)],
        compiler_params=pltpu.CompilerParams(vmem_limit_bytes=VMEM_LIMIT),
    )(phase)


def window_kernel(where, offsets, phase_all, amp_all, *rest):
    outs, (field, phase, amp, sems) = rest[:RING], rest[RING:]
    rank = where[0]

    def loads(layer, block):
        rows = half(block)
        return [
            pltpu.make_async_copy(
                source.at[layer, rows, :], target.at[layer, rows, :], sems.at[kind, layer, block]
            )
            for kind, source, target in ((0, phase_all, phase), (1, amp_all, amp))
        ]

    for layer in (0, 1):
        for block in range(3):
            for copy in loads(layer, block):
                copy.start()
    for layer in (0, 1):
        for block in range(3):
            for copy in loads(layer, block):
                copy.wait()
            for col in range(3):
                sine, cosine = sine_and_cosine(phase[layer, half(block), half(col)])
                size = amp[layer, half(block), half(col)]
                field[layer, 0, col, half(block), :] = size * cosine
                field[layer, 1, col, half(block), :] = size * sine
    lane = lax.broadcasted_iota(jnp.int32, (HALF, HALF), 1)
    for distance in range(RING):
        position = (rank + distance) % RING
        col_at = offsets[position, 1]
        turn = (HALF - col_at) % HALF
        inside = lane < HALF - col_at
        for parity in (0, 1):
            rows = pl.ds(offsets[position, 0] + parity, HALF, stride=2)
            for layer in (0, 1):
                for part in (0, 1):
                    turned = [
                        pltpu.roll(field[layer, part, col, rows, :], turn, 1) for col in range(3)
                    ]
                    target = outs[distance].at[layer]
                    for col in (0, 1):
                        target[parity, half(part), half(col)] = jnp.where(
                            inside, turned[col], turned[col + 1]
                        ).astype(BF)


def transmission_windows(where, offsets, phase, amp):
    shape = jax.ShapeDtypeStruct((2, 2, N, N), BF)
    return pl.pallas_call(
        window_kernel,
        name="windows",
        out_shape=[shape] * RING,
        in_specs=[SM, SM, ANY, ANY],
        out_specs=[VM] * RING,
        scratch_shapes=[
            pltpu.VMEM((2, 2, 3, PATCH, HALF), F32),
            pltpu.VMEM((2, PATCH, PATCH), F32),
            pltpu.VMEM((2, PATCH, PATCH), F32),
            pltpu.SemaphoreType.DMA((2, 2, 3)),
        ],
        compiler_params=pltpu.CompilerParams(vmem_limit_bytes=VMEM_LIMIT),
    )(where, offsets, in_hbm(phase), in_hbm(amp))


def chain_kernel(first, where, start, *rest):
    windows = rest[:RING]
    earlier = () if first else rest[RING : 2 * RING]
    rest = rest[RING + len(earlier) :]
    tables = rest[:5]
    count = RING + 1
    outs = rest[5 : 5 + count]
    trans, waves, middle, mixed, filtered, second, in_sems, out_sems = rest[5 + count :]
    rank = where[0]
    active = where[1] == 1 if first else where[1] == 0

    def window_load(distance, layer):
        slot = (rank + RING - distance) % RING
        source = windows[distance].at[layer]
        return pltpu.make_async_copy(source, trans.at[slot, layer], in_sems.at[slot, layer])

    def store(k):
        return pltpu.make_async_copy(waves.at[k], outs[k], out_sems.at[k])

    @pl.when(active)
    def _():
        begin_load = pltpu.make_async_copy(
            start, waves.at[(2 * RING - 1 - rank) % RING], in_sems.at[RING, 0]
        )
        begin_load.start()
        for distance in range(RING):
            for layer in (1, 0):
                window_load(distance, layer).start()
        begin_load.wait()

        def pair(step, carry):
            pair_at = RING - 1 - step
            slot = (pair_at + RING - rank) % RING
            for k in range(RING):

                @pl.when(slot == k)
                def _(k=k):
                    store(k).start()

            source = waves.at[slot]
            target = waves.at[
                jnp.where(pair_at == 0, RING, (pair_at + 2 * RING - 1 - rank) % RING)
            ]
            for layer, begin, end in ((1, source, middle), (0, middle, target)):

                def ready(layer=layer):
                    pltpu.make_async_copy(
                        windows[0].at[layer], trans.at[pair_at, layer], in_sems.at[pair_at, layer]
                    ).wait()

                def finish(parity, reals, imags, layer=layer, end=end):
                    for col in (0, 1):
                        tr = trans[pair_at, layer, parity, half(0), half(col)].astype(F32)
                        ti = trans[pair_at, layer, parity, half(1), half(col)].astype(F32)
                        qr, qi = reals[col], imags[col]
                        end[parity, half(0), half(col)] = (tr * qr + ti * qi).astype(BF)
                        end[parity, half(1), half(col)] = (tr * qi - ti * qr).astype(BF)

                back_step(begin, tables, mixed, filtered, second, finish, ready)
            return carry

        lax.fori_loop(0, RING, pair, 0)
        store(RING).start()
        for k in range(RING + 1):
            store(k).wait()

    if not first:

        @pl.when(jnp.logical_not(active))
        def _():
            copies = [
                pltpu.make_async_copy(earlier[k], outs[k], out_sems.at[k]) for k in range(RING)
            ]
            middle[...] = jnp.zeros_like(middle)
            copies.append(pltpu.make_async_copy(middle, outs[RING], out_sems.at[RING]))
            for copy in copies:
                copy.start()
            for copy in copies:
                copy.wait()


def run_chain(first, where, start, windows, earlier, tables):
    count = RING + 1
    wave = jax.ShapeDtypeStruct((2, N, N), BF)
    return pl.pallas_call(
        functools.partial(chain_kernel, first),
        name="chain_deep" if first else "chain_top",
        out_shape=[wave] * count,
        in_specs=[SM, ANY] + [ANY] * RING + [ANY] * len(earlier) + [VM] * 5,
        out_specs=[ANY] * count,
        scratch_shapes=[
            pltpu.VMEM((RING, 2, 2, N, N), BF),
            pltpu.VMEM((RING + 1, 2, N, N), BF),
            pltpu.VMEM((2, N, N), BF),
            *step_scratch(),
            pltpu.SemaphoreType.DMA((RING + 1, 2)),
            pltpu.SemaphoreType.DMA((RING + 1,)),
        ],
        compiler_params=pltpu.CompilerParams(vmem_limit_bytes=VMEM_LIMIT),
    )(where, start, *windows, *earlier, *tables)


def visit_kernel(index, where, offsets, entry_at, window_at, psi_at, *rest):
    tables = rest[:5]
    grads, entry, window, psi, middle, mixed, filtered, second, sems = rest[-9:]
    loads = [
        pltpu.make_async_copy(entry_at, entry, sems.at[0]),
        pltpu.make_async_copy(window_at.at[1], window, sems.at[1]),
        pltpu.make_async_copy(psi_at, psi, sems.at[2]),
    ]
    for copy in loads:
        copy.start()
    if index == 0:
        grads[...] = jnp.zeros_like(grads)
    lane = lax.broadcasted_iota(jnp.int32, (HALF, HALF), 1)
    position = (where[0] + RING - index) % RING
    col_at = offsets[position, 1]
    turn = col_at % HALF
    inside = lane >= col_at
    loads[0].wait()

    def ready():
        loads[1].wait()
        loads[2].wait()

    for layer in (1, 0):

        def finish(parity, reals, imags, layer=layer):
            terms = ([], [])
            for col in (0, 1):
                wr = psi[layer, parity, half(0), half(col)].astype(F32)
                wi = psi[layer, parity, half(1), half(col)].astype(F32)
                qr, qi = reals[col], imags[col]
                terms[0].append(pltpu.roll(wr * qr + wi * qi, turn, 1))
                terms[1].append(pltpu.roll(wr * qi - wi * qr, turn, 1))
                if layer == 1:
                    tr = window[parity, half(0), half(col)].astype(F32)
                    ti = window[parity, half(1), half(col)].astype(F32)
                    middle[parity, half(0), half(col)] = (tr * qr + ti * qi).astype(BF)
                    middle[parity, half(1), half(col)] = (tr * qi - ti * qr).astype(BF)
            rows = pl.ds(offsets[position, 0] + parity, HALF, stride=2)
            zero = jnp.zeros((HALF, HALF), F32)
            for part in (0, 1):
                left, right = terms[part]
                placed = (
                    jnp.where(inside, left, zero),
                    jnp.where(inside, right, left),
                    jnp.where(inside, zero, right),
                )
                for col in range(3):
                    grads[layer, part, col, rows, :] += placed[col]

        if layer == 1:
            back_step(entry, tables, mixed, filtered, second, finish, ready)
        else:
            back_step(middle, tables, mixed, filtered, second, finish)


def visit(index, where, offsets, entry, window, psi, tables, grads):
    earlier = () if index == 0 else (grads,)
    return pl.pallas_call(
        functools.partial(visit_kernel, index),
        name=f"visit_{index}",
        out_shape=jax.ShapeDtypeStruct((2, 2, 3, PATCH, HALF), F32),
        in_specs=[SM, SM] + [ANY] * 3 + [VM] * (5 + len(earlier)),
        out_specs=VM,
        scratch_shapes=[
            pltpu.VMEM((2, N, N), BF),
            pltpu.VMEM((2, N, N), BF),
            pltpu.VMEM((2, 2, N, N), BF),
            pltpu.VMEM((2, N, N), BF),
            *step_scratch(),
            pltpu.SemaphoreType.DMA((3,)),
        ],
        input_output_aliases={10: 0} if earlier else {},
        compiler_params=pltpu.CompilerParams(vmem_limit_bytes=VMEM_LIMIT),
    )(where, offsets, entry, in_hbm(window), in_hbm(psi), *tables, *earlier)


def pack_kernel(where, grads, probe, keep, send, summed):
    core, y_at = where[2], where[3]
    total = jnp.zeros((HALF, HALF), F32)
    for source in range(DEPTH):
        total = total + probe[source].astype(F32)
    summed[...] = total
    for distance in range(RING):
        for x_at in (0, 1):
            for out, core_at in ((keep, core), (send, 1 - core)):
                chunk = (x_at * RING + (y_at + distance) % RING) * 2 + core_at
                rows = pl.ds(pl.multiple_of(chunk * EACH, 8), EACH)
                own = pl.ds(pl.multiple_of(chunk * 8, 8), 8)
                for col in range(3):
                    pieces = [
                        grads[layer, part, col, rows, :] for layer in (0, 1) for part in (0, 1)
                    ]
                    pieces.append(summed[own, :] if col == 0 else jnp.zeros((8, HALF), F32))
                    pieces.append(jnp.zeros((8, HALF), F32))
                    out[distance, x_at, :, half(col)] = jnp.concatenate(pieces, 0).astype(BF)


def packed(where, grads, probe):
    shape = jax.ShapeDtypeStruct((RING, 2, CHUNK, PATCH), BF)
    return pl.pallas_call(
        pack_kernel,
        name="pack",
        out_shape=[shape, shape],
        in_specs=[SM, VM, VM],
        out_specs=[VM, VM],
        scratch_shapes=[pltpu.VMEM((HALF, HALF), F32)],
        compiler_params=pltpu.CompilerParams(vmem_limit_bytes=VMEM_LIMIT),
    )(where, grads, probe)


def core_sum_kernel(keep, arrived, *outs):
    for distance in range(RING):
        for x_at in (0, 1):
            total = keep[distance, x_at].astype(F32) + arrived[distance, x_at].astype(F32)
            outs[distance][x_at] = total.astype(BF)


def core_sum(keep, arrived):
    return pl.pallas_call(
        core_sum_kernel,
        name="core_sum",
        out_shape=[jax.ShapeDtypeStruct((2, CHUNK, PATCH), BF)] * RING,
        in_specs=[VM, VM],
        out_specs=[VM] * RING,
        compiler_params=pltpu.CompilerParams(vmem_limit_bytes=VMEM_LIMIT),
    )(keep, arrived)


def ring_sum_kernel(where, *rest):
    parts, (keep, send) = rest[:RING], rest[RING:]
    x_at = where[4]
    for out, which in ((keep, x_at), (send, 1 - x_at)):
        total = parts[0][which].astype(F32)
        for part in parts[1:]:
            total = total + part[which].astype(F32)
        out[...] = total.astype(out.dtype)


def ring_sum(where, parts):
    return pl.pallas_call(
        ring_sum_kernel,
        name="ring_sum",
        out_shape=[
            jax.ShapeDtypeStruct((CHUNK, PATCH), F32),
            jax.ShapeDtypeStruct((CHUNK, PATCH), BF),
        ],
        in_specs=[SM] + [VM] * RING,
        out_specs=[VM, VM],
        compiler_params=pltpu.CompilerParams(vmem_limit_bytes=VMEM_LIMIT),
    )(where, *parts)


def last_sum_kernel(keep, arrived, rows_out, probe_out):
    total = keep[...] + arrived[...].astype(F32)
    rows_out[...] = total[: 4 * EACH]
    probe_out[...] = total[4 * EACH : 4 * EACH + 8, :HALF]


def last_sum(keep, arrived):
    return pl.pallas_call(
        last_sum_kernel,
        name="last_sum",
        out_shape=[
            jax.ShapeDtypeStruct((4 * EACH, PATCH), F32),
            jax.ShapeDtypeStruct((8, HALF), F32),
        ],
        compiler_params=pltpu.CompilerParams(vmem_limit_bytes=VMEM_LIMIT),
    )(keep, arrived)


def moved(array, dx, dy, dc):
    route = [
        (8 * x + 2 * y + c, 8 * (x ^ dx) + 2 * ((y + dy) % RING) + (c ^ dc))
        for x in range(2)
        for y in range(RING)
        for c in range(2)
    ]
    return lax.ppermute(array, "probe", route)


def order_kernel(where, residual, saved, start, *rest):
    outs, (first, waves, done, sems, out_sems) = rest[:RING], rest[RING:]
    rank = where[0]
    loads = [pltpu.make_async_copy(residual.at[rank], first, sems.at[RING])]
    for index in range(RING):
        position = (rank + RING - index) % RING
        loads.append(
            pltpu.make_async_copy(saved.at[:, position], waves.at[index], sems.at[index])
        )
    for copy in loads:
        copy.start()
    rows = lax.broadcasted_iota(jnp.int32, (N, N), 0)
    cols = lax.broadcasted_iota(jnp.int32, (N, N), 1)
    take = (cols == 2 * (rows % HALF) + rows // HALF).astype(F32).astype(BF)

    def reorder(source, target):
        for part in (0, 1):
            ordered = dot(take, source[part]).astype(BF)
            for parity in (0, 1):
                target[parity, half(part), :] = ordered[half(parity), :]

    stores = []
    loads[0].wait()
    reorder(first, start)
    for index in range(RING):
        loads[1 + index].wait()
        for layer in (0, 1):
            reorder(waves.at[index, layer], done.at[index, layer])
        stores.append(pltpu.make_async_copy(done.at[index], outs[index], out_sems.at[index]))
        stores[-1].start()
    for copy in stores:
        copy.wait()


def row_parity_first(where, residual, saved):
    wave = (2, N, N)
    return pl.pallas_call(
        order_kernel,
        name="reorder",
        out_shape=[jax.ShapeDtypeStruct(wave, BF)]
        + [jax.ShapeDtypeStruct((2, *wave), BF)] * RING,
        in_specs=[SM, ANY, ANY],
        out_specs=[VM] + [pl.BlockSpec(memory_space=pltpu.HBM)] * RING,
        scratch_shapes=[
            pltpu.VMEM(wave, BF),
            pltpu.VMEM((RING, 2, *wave), BF),
            pltpu.VMEM((RING, 2, *wave), BF),
            pltpu.SemaphoreType.DMA((RING + 1,)),
            pltpu.SemaphoreType.DMA((RING,)),
        ],
        compiler_params=pltpu.CompilerParams(vmem_limit_bytes=VMEM_LIMIT),
    )(where, in_hbm(residual), in_hbm(saved))


def pieces_kernel(wave, pieces):
    width = N // DEPTH
    lane = lax.broadcasted_iota(jnp.int32, (HALF, HALF), 1) // width
    for piece in range(DEPTH):
        per_tile = HALF // width
        value = jnp.zeros((HALF, HALF), F32)
        for parity in (0, 1):
            for part in (0, 1):
                place = 2 * parity + part
                source = wave[parity, half(part), half(piece // per_tile)].astype(F32)
                shift = (place - piece % per_tile) * width % HALF
                moved = pltpu.roll(source, shift, 1) if shift else source
                value = jnp.where(lane == place, moved, value)
        pieces[piece] = value.astype(BF)


def column_pieces(wave):
    return pl.pallas_call(
        pieces_kernel,
        name="pieces",
        out_shape=jax.ShapeDtypeStruct((DEPTH, HALF, HALF), BF),
        compiler_params=pltpu.CompilerParams(vmem_limit_bytes=VMEM_LIMIT),
    )(wave)


def turned(array, distance):
    route = [
        (RING * ring + i, RING * ring + (i + distance) % RING)
        for ring in range(2)
        for i in range(RING)
    ]
    return lax.ppermute(array, "depth", route)


def exchanged(arrays):
    return [arrays[0]] + [turned(arrays[k], k) for k in range(1, RING)]


def shards(residual, saved_waves, object_phase, object_amp, prop_phase, offsets):
    depth_at = lax.axis_index("depth")
    probe_at = lax.axis_index("probe")
    where = jnp.stack(
        [depth_at % RING, depth_at // RING, probe_at % 2, probe_at // 2 % RING, probe_at // 8]
    ).astype(jnp.int32)
    own = transmission_windows(where, offsets, object_phase, object_amp)
    tables = (*transform_tables(N), *filters(prop_phase))
    start, *waves = row_parity_first(where, residual, saved_waves)
    foreign = exchanged(own)
    *deep, leaving = run_chain(True, where, start, foreign, (), tables)
    arrived = lax.ppermute(leaving, "depth", [(RING + i, i) for i in range(RING)])
    *entries, ending = run_chain(False, where, arrived, foreign, deep, tables)
    entries = exchanged(entries)
    grads = None
    for index in (0, 3, 1, 2):
        window = own[(RING - index) % RING]
        grads = visit(
            index, where, offsets, entries[index], window, waves[index], tables, grads
        )
        if index == 0:
            ending, grads = lax.optimization_barrier((ending, grads))
            probe = lax.all_to_all(column_pieces(ending), "depth", 0, 0, tiled=True)
    keep, send = packed(where, grads, probe)
    parts = list(core_sum(keep, moved(send, 0, 0, 1)))
    parts = parts[:1] + [moved(parts[k], 0, k, 0) for k in range(1, RING)]
    keep, send = ring_sum(where, parts)
    rows, probe_rows = last_sum(keep, moved(send, 1, 0, 0))
    object_grad = rows.reshape(2, 2, EACH, PATCH)
    probe_grad = probe_rows.reshape(8, 2, 2, N // DEPTH).transpose(2, 0, 1, 3)
    return (object_grad, probe_grad.reshape(2, 16, N // DEPTH))


def solution(mesh):
    return jax.shard_map(
        shards,
        mesh=mesh,
        in_specs=(
            P("probe", None, None, None),
            P("depth", "probe", None, None, None),
            P("depth", None, None),
            P("depth", None, None),
            P(),
            P("probe", None),
        ),
        out_specs=(P("depth", None, "probe", None), P(None, "probe", "depth")),
        check_vma=False,
    )
```

```python
import functools
import math

import jax
import jax.numpy as jnp
from jax import lax
from jax.experimental import pallas as pl
from jax.experimental.pallas import tpu as pltpu
from jax.sharding import PartitionSpec as P

BF = jnp.bfloat16
F32 = jnp.float32
RING = 4
DEPTH = 8
N = 256
HALF = 128
PATCH = 384
EACH = PATCH // 16
CHUNK = 4 * EACH + 16
ANY = pl.BlockSpec(memory_space=pl.ANY)
VM = pl.BlockSpec(memory_space=pltpu.VMEM)
SM = pl.BlockSpec(memory_space=pltpu.SMEM)
SINE = (0.999999995716, -0.166666579699, 0.00833305061733, -0.000198090463574, 2.60516627618e-06)
COSINE = (0.99999999978, -0.49999999357, 0.0416666362089, -0.00138883608423, 2.47601355058e-05, -2.60510761786e-07)
VMEM_LIMIT = 20 * 1024 * 1024


def in_hbm(array):
    return pltpu.with_memory_space_constraint(array, pltpu.HBM)


def half(index):
    return slice(index * HALF, (index + 1) * HALF)


def dot(a, b):
    return jnp.dot(a, b, preferred_element_type=F32)


def back_step(source, tables, mixed, filtered, second, finish, ready=None):
    inward, table, flipped, kernel_cos, kernel_sin = tables
    for part in (0, 1):
        even = dot(inward[0, half(part), :], source[0])
        odd = dot(inward[1, half(part), :], source[1])
        for row, value in ((0, even + odd), (1, even - odd)):
            left, right = value[:, :HALF], value[:, HALF:]
            mixed[0, half(row), half(part)] = (left + right).astype(BF)
            mixed[1, half(row), half(part)] = (left - right).astype(BF)
    for col in (0, 1):
        upper = dot(mixed[col, half(0), :], flipped[col])
        lower = dot(mixed[col, half(1), :], flipped[col])
        for parity in (0, 1):
            real = upper[:, half(parity)]
            imag = lower[:, half(parity)]
            kc = kernel_cos[half(parity), half(col)]
            ks = kernel_sin[half(parity), half(col)]
            filtered[parity, half(0), half(col)] = (kc * real + ks * imag).astype(BF)
            filtered[parity, half(1), half(col)] = (kc * imag - ks * real).astype(BF)
    for part in (0, 1):
        even = dot(flipped[0, half(part), :], filtered[0])
        odd = dot(flipped[1, half(part), :], filtered[1])
        total = (even + odd).astype(BF)
        diff = (even - odd).astype(BF)
        for col in (0, 1):
            second[col, half(0), half(part)] = total[:, half(col)]
            second[col, half(1), half(part)] = diff[:, half(col)]
    if ready is not None:
        ready()
    totals, diffs = [], []
    for row in (0, 1):
        even = dot(second[0, half(row), :], table[0])
        odd = dot(second[1, half(row), :], table[1])
        totals.append(even + odd)
        diffs.append(even - odd)
    for parity in (0, 1):
        finish(
            parity,
            (totals[0][:, half(parity)], diffs[0][:, half(parity)]),
            (totals[1][:, half(parity)], diffs[1][:, half(parity)]),
        )


def step_scratch():
    return [pltpu.VMEM((2, N, N), BF), pltpu.VMEM((2, N, N), BF), pltpu.VMEM((2, N, N), BF)]


def sine_and_cosine(angle):
    half_angle = 0.5 * angle
    square = half_angle * half_angle

    def series(factors):
        value = jnp.full_like(square, factors[-1])
        for factor in factors[-2::-1]:
            value = value * square + factor
        return value

    low_sine = half_angle * series(SINE)
    low_cosine = series(COSINE)
    return 2.0 * low_sine * low_cosine, 1.0 - 2.0 * low_sine * low_sine


def write_tables(inward, table, flipped):
    first = lax.broadcasted_iota(jnp.int32, (HALF, HALF), 0)
    second = lax.broadcasted_iota(jnp.int32, (HALF, HALF), 1)
    factor = 1.0 / math.sqrt(N)
    for spread, other, targets in (
        (second, first, ((inward, 1.0), (flipped, -1.0))),
        (first, second, ((table, 1.0),)),
    ):
        for parity in (0, 1):
            order = (2 * spread + parity) * other % N
            order = jnp.where(order > HALF, order - N, order)
            sine, cosine = sine_and_cosine(2.0 * math.pi / N * order.astype(F32))
            for target, sign in targets:
                for row in (0, 1):
                    target[parity, half(row), half(row)] = (cosine * factor).astype(BF)
                    turned_sine = sine * (factor * (sign if row == 0 else -sign))
                    target[parity, half(row), half(1 - row)] = turned_sine.astype(BF)


def filter_kernel(phase, inward, table, flipped, kernel_cos, kernel_sin, plain):
    write_tables(inward, table, flipped)
    rows = lax.broadcasted_iota(jnp.int32, (N, N), 0)
    cols = lax.broadcasted_iota(jnp.int32, (N, N), 1)
    take = (rows == 2 * (cols % HALF) + cols // HALF).astype(F32).astype(BF)
    for col in (0, 1):
        sine, cosine = sine_and_cosine(phase[:, half(col)])
        plain[0, col] = cosine
        plain[1, col] = sine
    for index, out in ((0, kernel_cos), (1, kernel_sin)):
        for parity in (0, 1):
            picked = [plain[index, col, pl.ds(parity, HALF, stride=2), :] for col in (0, 1)]
            rest = jnp.concatenate(picked, 1)
            value = jnp.zeros((HALF, N), F32)
            for _ in range(3):
                term = rest.astype(BF)
                value = value + dot(term, take)
                rest = rest - term.astype(F32)
            out[half(parity), :] = value


def filters(phase):
    shape = jax.ShapeDtypeStruct((N, N), F32)
    pair = jax.ShapeDtypeStruct((2, N, N), BF)
    return pl.pallas_call(
        filter_kernel,
        name="filters",
        out_shape=[pair, pair, pair, shape, shape],
        in_specs=[VM],
        out_specs=[VM] * 5,
        scratch_shapes=[pltpu.VMEM((2, 2, N, HALF), F32)],
        compiler_params=pltpu.CompilerParams(vmem_limit_bytes=VMEM_LIMIT),
    )(phase)


def window_kernel(where, offsets, phase_all, amp_all, *rest):
    outs, (field, phase, amp, sems) = rest[:RING], rest[RING:]
    rank = where[0]

    def loads(layer, block):
        rows = half(block)
        return [
            pltpu.make_async_copy(
                source.at[layer, rows, :], target.at[layer, rows, :], sems.at[kind, layer, block]
            )
            for kind, source, target in ((0, phase_all, phase), (1, amp_all, amp))
        ]

    for layer in (0, 1):
        for block in range(3):
            for copy in loads(layer, block):
                copy.start()
    for layer in (0, 1):
        for block in range(3):
            for copy in loads(layer, block):
                copy.wait()
            for col in range(3):
                sine, cosine = sine_and_cosine(phase[layer, half(block), half(col)])
                size = amp[layer, half(block), half(col)]
                field[layer, 0, col, half(block), :] = size * cosine
                field[layer, 1, col, half(block), :] = size * sine
    lane = lax.broadcasted_iota(jnp.int32, (HALF, HALF), 1)
    for distance in range(RING):
        position = (rank + distance) % RING
        col_at = offsets[position, 1]
        turn = (HALF - col_at) % HALF
        inside = lane < HALF - col_at
        for parity in (0, 1):
            rows = pl.ds(offsets[position, 0] + parity, HALF, stride=2)
            for layer in (0, 1):
                for part in (0, 1):
                    turned = [
                        pltpu.roll(field[layer, part, col, rows, :], turn, 1) for col in range(3)
                    ]
                    target = outs[distance].at[layer]
                    for col in (0, 1):
                        target[parity, half(part), half(col)] = jnp.where(
                            inside, turned[col], turned[col + 1]
                        ).astype(BF)


def transmission_windows(where, offsets, phase, amp):
    shape = jax.ShapeDtypeStruct((2, 2, N, N), BF)
    return pl.pallas_call(
        window_kernel,
        name="windows",
        out_shape=[shape] * RING,
        in_specs=[SM, SM, ANY, ANY],
        out_specs=[VM] * RING,
        scratch_shapes=[
            pltpu.VMEM((2, 2, 3, PATCH, HALF), F32),
            pltpu.VMEM((2, PATCH, PATCH), F32),
            pltpu.VMEM((2, PATCH, PATCH), F32),
            pltpu.SemaphoreType.DMA((2, 2, 3)),
        ],
        compiler_params=pltpu.CompilerParams(vmem_limit_bytes=VMEM_LIMIT),
    )(where, offsets, in_hbm(phase), in_hbm(amp))


def column_pieces(wave, place_at, target):
    width = N // DEPTH
    lane = lax.broadcasted_iota(jnp.int32, (HALF, HALF), 1) // width
    for far in (0, 1):
        value = jnp.zeros((HALF, HALF), F32)
        for parity in (0, 1):
            for part in (0, 1):
                place = 2 * parity + part
                source = wave[parity, half(part), half(far)].astype(F32)
                turn = (place + RING - place_at) % RING * width
                value = jnp.where(lane == place, pltpu.roll(source, turn, 1), value)
        target[:, half(far)] = value.astype(BF)


def chain_kernel(first, where, start, *rest):
    count = RING + 1 if first else RING
    windows = rest[: RING + 1]
    earlier = () if first else rest[RING + 1 : 2 * RING + 1]
    rest = rest[RING + 1 + len(earlier) :]
    tables = rest[:5]
    outs = rest[5 : 5 + count]
    trans, waves, middle, mixed, filtered, second = rest[5 + count :]
    rank = where[0]
    active = where[1] == 1 if first else where[1] == 0
    inner = jnp.logical_or(rank == 1, rank == 2)

    @pl.when(active)
    def _():
        for parity in (0, 1):
            waves[(2 * RING - 1 - rank) % RING, parity] = start[parity * N : (parity + 1) * N, :]

        def pair(step, carry):
            pair_at = RING - 1 - step
            slot = (pair_at + RING - rank) % RING
            for k in range(RING):

                @pl.when(slot == k)
                def _(k=k):
                    for parity in (0, 1):
                        outs[k][parity * N : (parity + 1) * N, :] = waves[k, parity]

            source = waves.at[slot]
            target = waves.at[
                jnp.where(pair_at == 0, RING, (pair_at + 2 * RING - 1 - rank) % RING)
            ]
            for layer, begin, end in ((1, source, middle), (0, middle, target)):

                def ready(layer=layer):
                    distance = (rank + RING - pair_at) % RING
                    index = jnp.where(
                        jnp.logical_and(distance == 2, jnp.logical_not(inner)), RING, distance
                    )
                    for k in range(RING + 1):

                        @pl.when(index == k)
                        def _(k=k):
                            for parity in (0, 1):
                                trans[parity] = windows[k][layer, parity]

                def finish(parity, reals, imags, layer=layer, end=end):
                    for col in (0, 1):
                        tr = trans[parity, half(0), half(col)].astype(F32)
                        ti = trans[parity, half(1), half(col)].astype(F32)
                        qr, qi = reals[col], imags[col]
                        end[parity, half(0), half(col)] = (tr * qr + ti * qi).astype(BF)
                        end[parity, half(1), half(col)] = (tr * qi - ti * qr).astype(BF)

                back_step(begin, tables, mixed, filtered, second, finish, ready)
            return carry

        lax.fori_loop(0, RING, pair, 0)
        if first:
            for parity in (0, 1):
                outs[RING][parity * N : (parity + 1) * N, :] = waves[RING, parity]
        else:
            for k in range(RING):
                column_pieces(waves.at[RING], (rank + k) % RING, outs[k].at[2 * N :])

    if not first:

        @pl.when(jnp.logical_not(active))
        def _():
            for k in range(RING):
                outs[k][: 2 * N, :] = earlier[k][...]
                outs[k][2 * N :, :] = jnp.zeros((HALF, N), BF)


def run_chain(first, where, start, windows, earlier, tables):
    count = RING + 1 if first else RING
    wave = jax.ShapeDtypeStruct((2 * N if first else 2 * N + HALF, N), BF)
    return pl.pallas_call(
        functools.partial(chain_kernel, first),
        name="chain_deep" if first else "chain_top",
        out_shape=[wave] * count,
        in_specs=[SM] + [VM] * (RING + 7 + len(earlier)),
        out_specs=[VM] * count,
        scratch_shapes=[
            pltpu.VMEM((2, N, N), BF),
            pltpu.VMEM((RING + 1, 2, N, N), BF),
            pltpu.VMEM((2, N, N), BF),
            *step_scratch(),
        ],
        compiler_params=pltpu.CompilerParams(vmem_limit_bytes=VMEM_LIMIT),
    )(where, start, *windows, *earlier, *tables)


def visit_kernel(index, where, offsets, entry, window, psi, *rest):
    tables = rest[:5]
    grads, middle, mixed, filtered, second = rest[-5:]
    if index == 0:
        grads[...] = jnp.zeros_like(grads)
    lane = lax.broadcasted_iota(jnp.int32, (HALF, HALF), 1)
    position = (where[0] + RING - index) % RING
    col_at = offsets[position, 1]
    turn = col_at % HALF
    inside = lane >= col_at

    for layer in (1, 0):

        def finish(parity, reals, imags, layer=layer):
            terms = ([], [])
            for col in (0, 1):
                wr = psi[layer, parity, half(0), half(col)].astype(F32)
                wi = psi[layer, parity, half(1), half(col)].astype(F32)
                qr, qi = reals[col], imags[col]
                terms[0].append(pltpu.roll(wr * qr + wi * qi, turn, 1))
                terms[1].append(pltpu.roll(wr * qi - wi * qr, turn, 1))
                if layer == 1:
                    tr = window[layer, parity, half(0), half(col)].astype(F32)
                    ti = window[layer, parity, half(1), half(col)].astype(F32)
                    middle[parity, half(0), half(col)] = (tr * qr + ti * qi).astype(BF)
                    middle[parity, half(1), half(col)] = (tr * qi - ti * qr).astype(BF)
            rows = pl.ds(offsets[position, 0] + parity, HALF, stride=2)
            zero = jnp.zeros((HALF, HALF), F32)
            for part in (0, 1):
                left, right = terms[part]
                placed = (
                    jnp.where(inside, left, zero),
                    jnp.where(inside, right, left),
                    jnp.where(inside, zero, right),
                )
                for col in range(3):
                    grads[layer, part, col, rows, :] += placed[col]

        if layer == 1:
            waves = (entry[:N, :], entry[N : 2 * N, :])
            back_step(waves, tables, mixed, filtered, second, finish)
        else:
            back_step(middle, tables, mixed, filtered, second, finish)


def visit(index, where, offsets, entry, window, psi, tables, grads):
    earlier = () if index == 0 else (grads,)
    return pl.pallas_call(
        functools.partial(visit_kernel, index),
        name=f"visit_{index}",
        out_shape=jax.ShapeDtypeStruct((2, 2, 3, PATCH, HALF), F32),
        in_specs=[SM, SM] + [VM] * (8 + len(earlier)),
        out_specs=VM,
        scratch_shapes=[
            pltpu.VMEM((2, N, N), BF),
            *step_scratch(),
        ],
        input_output_aliases={10: 0} if earlier else {},
        compiler_params=pltpu.CompilerParams(vmem_limit_bytes=VMEM_LIMIT),
    )(where, offsets, entry, window, psi, *tables, *earlier)


def probe_sum_kernel(*refs):
    entries, (own, other) = refs[:RING], refs[RING:]
    total = entries[0][2 * N :, :].astype(F32)
    for entry in entries[1:]:
        total = total + entry[2 * N :, :].astype(F32)
    own[...] = total[:, :HALF].astype(BF)
    other[...] = total[:, HALF:].astype(BF)


def probe_sum(entries):
    shape = jax.ShapeDtypeStruct((HALF, HALF), BF)
    return pl.pallas_call(
        probe_sum_kernel,
        name="probe_sum",
        out_shape=[shape, shape],
        in_specs=[VM] * RING,
        out_specs=[VM, VM],
        compiler_params=pltpu.CompilerParams(vmem_limit_bytes=VMEM_LIMIT),
    )(*entries)


def pack_kernel(where, grads, own_probe, far_probe, keep, send, summed):
    core, y_at = where[2], where[3]

    @pl.when(where[1] == 0)
    def _():
        summed[...] = own_probe[...].astype(F32)

    @pl.when(where[1] == 1)
    def _():
        summed[...] = far_probe[...].astype(F32)

    for distance in range(RING):
        for x_at in (0, 1):
            for out, core_at in ((keep, core), (send, 1 - core)):
                chunk = (x_at * RING + (y_at + distance) % RING) * 2 + core_at
                rows = pl.ds(pl.multiple_of(chunk * EACH, 8), EACH)
                own = pl.ds(pl.multiple_of(chunk * 8, 8), 8)
                for col in range(3):
                    pieces = [
                        grads[layer, part, col, rows, :] for layer in (0, 1) for part in (0, 1)
                    ]
                    pieces.append(summed[own, :] if col == 0 else jnp.zeros((8, HALF), F32))
                    pieces.append(jnp.zeros((8, HALF), F32))
                    out[distance, x_at, :, half(col)] = jnp.concatenate(pieces, 0).astype(BF)


def packed(where, grads, own_probe, far_probe):
    shape = jax.ShapeDtypeStruct((RING, 2, CHUNK, PATCH), BF)
    return pl.pallas_call(
        pack_kernel,
        name="pack",
        out_shape=[shape, shape],
        in_specs=[SM, VM, VM, VM],
        out_specs=[VM, VM],
        scratch_shapes=[pltpu.VMEM((HALF, HALF), F32)],
        compiler_params=pltpu.CompilerParams(vmem_limit_bytes=VMEM_LIMIT),
    )(where, grads, own_probe, far_probe)


def core_sum_kernel(keep, arrived, *outs):
    for distance in range(RING):
        for x_at in (0, 1):
            total = keep[distance, x_at].astype(F32) + arrived[distance, x_at].astype(F32)
            outs[distance][x_at] = total.astype(BF)


def core_sum(keep, arrived):
    return pl.pallas_call(
        core_sum_kernel,
        name="core_sum",
        out_shape=[jax.ShapeDtypeStruct((2, CHUNK, PATCH), BF)] * RING,
        in_specs=[VM, VM],
        out_specs=[VM] * RING,
        compiler_params=pltpu.CompilerParams(vmem_limit_bytes=VMEM_LIMIT),
    )(keep, arrived)


def ring_sum_kernel(where, *rest):
    parts, (keep, send) = rest[:RING], rest[RING:]
    x_at = where[4]
    for out, which in ((keep, x_at), (send, 1 - x_at)):
        total = parts[0][which].astype(F32)
        for part in parts[1:]:
            total = total + part[which].astype(F32)
        out[...] = total.astype(out.dtype)


def ring_sum(where, parts):
    return pl.pallas_call(
        ring_sum_kernel,
        name="ring_sum",
        out_shape=[
            jax.ShapeDtypeStruct((CHUNK, PATCH), F32),
            jax.ShapeDtypeStruct((CHUNK, PATCH), BF),
        ],
        in_specs=[SM] + [VM] * RING,
        out_specs=[VM, VM],
        compiler_params=pltpu.CompilerParams(vmem_limit_bytes=VMEM_LIMIT),
    )(where, *parts)


def last_sum_kernel(keep, arrived, rows_out, probe_out):
    total = keep[...] + arrived[...].astype(F32)
    rows_out[...] = total[: 4 * EACH]
    probe_out[...] = total[4 * EACH : 4 * EACH + 8, :HALF]


def last_sum(keep, arrived):
    return pl.pallas_call(
        last_sum_kernel,
        name="last_sum",
        out_shape=[
            jax.ShapeDtypeStruct((4 * EACH, PATCH), F32),
            jax.ShapeDtypeStruct((8, HALF), F32),
        ],
        compiler_params=pltpu.CompilerParams(vmem_limit_bytes=VMEM_LIMIT),
    )(keep, arrived)


def moved(array, dx, dy, dc):
    route = [
        (8 * x + 2 * y + c, 8 * (x ^ dx) + 2 * ((y + dy) % RING) + (c ^ dc))
        for x in range(2)
        for y in range(RING)
        for c in range(2)
    ]
    return lax.ppermute(array, "probe", route)


def order_kernel(where, residual, saved, start, *rest):
    outs, (first, begin, waves, sems) = rest[:RING], rest[RING:]
    rank = where[0]
    loads = [pltpu.make_async_copy(residual.at[rank], first, sems.at[RING])]
    for index in range(RING):
        position = (rank + RING - index) % RING
        loads.append(
            pltpu.make_async_copy(saved.at[:, position], waves.at[index], sems.at[index])
        )
    for copy in loads:
        copy.start()
    rows = lax.broadcasted_iota(jnp.int32, (N, N), 0)
    cols = lax.broadcasted_iota(jnp.int32, (N, N), 1)
    take = (cols == 2 * (rows % HALF) + rows // HALF).astype(F32).astype(BF)

    def reorder(source, target):
        for part in (0, 1):
            ordered = dot(take, source[part]).astype(BF)
            for parity in (0, 1):
                target[parity, half(part), :] = ordered[half(parity), :]

    loads[0].wait()
    reorder(first, begin)
    for parity in (0, 1):
        start[parity * N : (parity + 1) * N, :] = begin[parity]
    for index in range(RING):
        loads[1 + index].wait()
        for layer in (0, 1):
            reorder(waves.at[index, layer], outs[index].at[layer])


def row_parity_first(where, residual, saved):
    wave = (2, N, N)
    return pl.pallas_call(
        order_kernel,
        name="reorder",
        out_shape=[jax.ShapeDtypeStruct((2 * N, N), BF)]
        + [jax.ShapeDtypeStruct((2, *wave), BF)] * RING,
        in_specs=[SM, ANY, ANY],
        out_specs=[VM] * (RING + 1),
        scratch_shapes=[
            pltpu.VMEM(wave, BF),
            pltpu.VMEM(wave, BF),
            pltpu.VMEM((RING, 2, *wave), BF),
            pltpu.SemaphoreType.DMA((RING + 1,)),
        ],
        compiler_params=pltpu.CompilerParams(vmem_limit_bytes=VMEM_LIMIT),
    )(where, in_hbm(residual), in_hbm(saved))


def turned(array, distance):
    route = [
        (RING * ring + i, RING * ring + (i + distance) % RING)
        for ring in range(2)
        for i in range(RING)
    ]
    return lax.ppermute(array, "depth", route)


def exchanged(arrays):
    return [arrays[0]] + [turned(arrays[k], k) for k in range(1, RING)]


def ring_route(*pairs):
    return [(RING * ring + a, RING * ring + b) for ring in range(2) for a, b in pairs]


def exchanged_windows(own):
    relay = lax.ppermute(own[2], "depth", ring_route((1, 0), (2, 3)))
    far = lax.ppermute(own[2], "depth", ring_route((0, 2), (3, 1)))
    ahead = turned(own[1], 1)
    back = turned(own[3], 3)
    return [own[0], ahead, far, back, lax.ppermute(relay, "depth", ring_route((0, 3), (3, 0)))]


def shards(residual, saved_waves, object_phase, object_amp, prop_phase, offsets):
    depth_at = lax.axis_index("depth")
    probe_at = lax.axis_index("probe")
    where = jnp.stack(
        [depth_at % RING, depth_at // RING, probe_at % 2, probe_at // 2 % RING, probe_at // 8]
    ).astype(jnp.int32)
    own = transmission_windows(where, offsets, object_phase, object_amp)
    tables = filters(prop_phase)
    start, *waves = row_parity_first(where, residual, saved_waves)
    foreign = exchanged_windows(own)
    *deep, leaving = run_chain(True, where, start, foreign, (), tables)
    arrived = lax.ppermute(leaving, "depth", [(RING + i, i) for i in range(RING)])
    entries = exchanged(run_chain(False, where, arrived, foreign, deep, tables))
    grads = None
    for index in (0, 3, 1, 2):
        if index == 2:
            *entries, grads = lax.optimization_barrier((*entries, grads))
            own_probe, other_probe = probe_sum(entries)
            far_probe = lax.ppermute(other_probe, "depth", [(i, RING + i) for i in range(RING)])
        window = own[(RING - index) % RING]
        grads = visit(
            index, where, offsets, entries[index], window, waves[index], tables, grads
        )
    keep, send = packed(where, grads, own_probe, far_probe)
    parts = list(core_sum(keep, moved(send, 0, 0, 1)))
    parts = parts[:1] + [moved(parts[k], 0, k, 0) for k in range(1, RING)]
    keep, send = ring_sum(where, parts)
    rows, probe_rows = last_sum(keep, moved(send, 1, 0, 0))
    object_grad = rows.reshape(2, 2, EACH, PATCH)
    probe_grad = probe_rows.reshape(8, 2, 2, N // DEPTH).transpose(2, 0, 1, 3)
    return (object_grad, probe_grad.reshape(2, 16, N // DEPTH))


def solution(mesh):
    return jax.shard_map(
        shards,
        mesh=mesh,
        in_specs=(
            P("probe", None, None, None),
            P("depth", "probe", None, None, None),
            P("depth", None, None),
            P("depth", None, None),
            P(),
            P("probe", None),
        ),
        out_specs=(P("depth", None, "probe", None), P(None, "probe", "depth")),
        check_vma=False,
    )
```

```python
import functools
import math

import jax
import jax.numpy as jnp
from jax import lax
from jax.experimental import pallas as pl
from jax.experimental.pallas import tpu as pltpu
from jax.sharding import PartitionSpec as P

BF = jnp.bfloat16
F32 = jnp.float32
RING = 4
DEPTH = 8
N = 256
HALF = 128
PATCH = 384
EACH = PATCH // 16
CHUNK = 4 * EACH + 16
ANY = pl.BlockSpec(memory_space=pl.ANY)
VM = pl.BlockSpec(memory_space=pltpu.VMEM)
SM = pl.BlockSpec(memory_space=pltpu.SMEM)
SINE = (0.999999995716, -0.166666579699, 0.00833305061733, -0.000198090463574, 2.60516627618e-06)
COSINE = (0.99999999978, -0.49999999357, 0.0416666362089, -0.00138883608423, 2.47601355058e-05, -2.60510761786e-07)
VMEM_LIMIT = 20 * 1024 * 1024


def in_hbm(array):
    return pltpu.with_memory_space_constraint(array, pltpu.HBM)


def half(index):
    return slice(index * HALF, (index + 1) * HALF)


def dot(a, b):
    return jnp.dot(a, b, preferred_element_type=F32)


def back_step(source, tables, mixed, filtered, second, finish, ready=None):
    inward, table, flipped, kernel_cos, kernel_sin = tables
    for part in (0, 1):
        even = dot(inward[0, half(part), :], source[0])
        odd = dot(inward[1, half(part), :], source[1])
        for row, value in ((0, even + odd), (1, even - odd)):
            left, right = value[:, :HALF], value[:, HALF:]
            mixed[0, half(row), half(part)] = (left + right).astype(BF)
            mixed[1, half(row), half(part)] = (left - right).astype(BF)
    for col in (0, 1):
        upper = dot(mixed[col, half(0), :], flipped[col])
        lower = dot(mixed[col, half(1), :], flipped[col])
        for parity in (0, 1):
            real = upper[:, half(parity)]
            imag = lower[:, half(parity)]
            kc = kernel_cos[half(parity), half(col)]
            ks = kernel_sin[half(parity), half(col)]
            filtered[parity, half(0), half(col)] = (kc * real + ks * imag).astype(BF)
            filtered[parity, half(1), half(col)] = (kc * imag - ks * real).astype(BF)
    for part in (0, 1):
        even = dot(flipped[0, half(part), :], filtered[0])
        odd = dot(flipped[1, half(part), :], filtered[1])
        total = (even + odd).astype(BF)
        diff = (even - odd).astype(BF)
        for col in (0, 1):
            second[col, half(0), half(part)] = total[:, half(col)]
            second[col, half(1), half(part)] = diff[:, half(col)]
    if ready is not None:
        ready()
    totals, diffs = [], []
    for row in (0, 1):
        even = dot(second[0, half(row), :], table[0])
        odd = dot(second[1, half(row), :], table[1])
        totals.append(even + odd)
        diffs.append(even - odd)
    for parity in (0, 1):
        finish(
            parity,
            (totals[0][:, half(parity)], diffs[0][:, half(parity)]),
            (totals[1][:, half(parity)], diffs[1][:, half(parity)]),
        )


def step_scratch():
    return [pltpu.VMEM((2, N, N), BF), pltpu.VMEM((2, N, N), BF), pltpu.VMEM((2, N, N), BF)]


def sine_and_cosine(angle):
    half_angle = 0.5 * angle
    square = half_angle * half_angle

    def series(factors):
        value = jnp.full_like(square, factors[-1])
        for factor in factors[-2::-1]:
            value = value * square + factor
        return value

    low_sine = half_angle * series(SINE)
    low_cosine = series(COSINE)
    return 2.0 * low_sine * low_cosine, 1.0 - 2.0 * low_sine * low_sine


def write_tables(inward, table, flipped):
    first = lax.broadcasted_iota(jnp.int32, (HALF, HALF), 0)
    second = lax.broadcasted_iota(jnp.int32, (HALF, HALF), 1)
    factor = 1.0 / math.sqrt(N)
    for spread, other, targets in (
        (second, first, ((inward, 1.0), (flipped, -1.0))),
        (first, second, ((table, 1.0),)),
    ):
        for parity in (0, 1):
            order = (2 * spread + parity) * other % N
            order = jnp.where(order > HALF, order - N, order)
            sine, cosine = sine_and_cosine(2.0 * math.pi / N * order.astype(F32))
            for target, sign in targets:
                for row in (0, 1):
                    target[parity, half(row), half(row)] = (cosine * factor).astype(BF)
                    turned_sine = sine * (factor * (sign if row == 0 else -sign))
                    target[parity, half(row), half(1 - row)] = turned_sine.astype(BF)


def filter_kernel(phase, inward, table, flipped, kernel_cos, kernel_sin, plain):
    write_tables(inward, table, flipped)
    rows = lax.broadcasted_iota(jnp.int32, (N, N), 0)
    cols = lax.broadcasted_iota(jnp.int32, (N, N), 1)
    take = (rows == 2 * (cols % HALF) + cols // HALF).astype(F32).astype(BF)
    for col in (0, 1):
        sine, cosine = sine_and_cosine(phase[:, half(col)])
        plain[0, col] = cosine
        plain[1, col] = sine
    for index, out in ((0, kernel_cos), (1, kernel_sin)):
        for parity in (0, 1):
            picked = [plain[index, col, pl.ds(parity, HALF, stride=2), :] for col in (0, 1)]
            rest = jnp.concatenate(picked, 1)
            value = jnp.zeros((HALF, N), F32)
            for _ in range(3):
                term = rest.astype(BF)
                value = value + dot(term, take)
                rest = rest - term.astype(F32)
            out[half(parity), :] = value


def filters(phase):
    shape = jax.ShapeDtypeStruct((N, N), F32)
    pair = jax.ShapeDtypeStruct((2, N, N), BF)
    return pl.pallas_call(
        filter_kernel,
        name="filters",
        out_shape=[pair, pair, pair, shape, shape],
        in_specs=[VM],
        out_specs=[VM] * 5,
        scratch_shapes=[pltpu.VMEM((2, 2, N, HALF), F32)],
        compiler_params=pltpu.CompilerParams(vmem_limit_bytes=VMEM_LIMIT),
    )(phase)


def window_kernel(where, offsets, phase_all, amp_all, *rest):
    outs, (field, phase, amp, sems) = rest[:RING], rest[RING:]
    rank = where[0]

    def loads(layer, block):
        rows = half(block)
        return [
            pltpu.make_async_copy(
                source.at[layer, rows, :], target.at[layer, rows, :], sems.at[kind, layer, block]
            )
            for kind, source, target in ((0, phase_all, phase), (1, amp_all, amp))
        ]

    for layer in (0, 1):
        for block in range(3):
            for copy in loads(layer, block):
                copy.start()
    for layer in (0, 1):
        for block in range(3):
            for copy in loads(layer, block):
                copy.wait()
            for col in range(3):
                sine, cosine = sine_and_cosine(phase[layer, half(block), half(col)])
                size = amp[layer, half(block), half(col)]
                field[layer, 0, col, half(block), :] = size * cosine
                field[layer, 1, col, half(block), :] = size * sine
    lane = lax.broadcasted_iota(jnp.int32, (HALF, HALF), 1)
    for distance in range(RING):
        position = (rank + distance) % RING
        col_at = offsets[position, 1]
        turn = (HALF - col_at) % HALF
        inside = lane < HALF - col_at
        for parity in (0, 1):
            rows = pl.ds(offsets[position, 0] + parity, HALF, stride=2)
            for layer in (0, 1):
                for part in (0, 1):
                    turned = [
                        pltpu.roll(field[layer, part, col, rows, :], turn, 1) for col in range(3)
                    ]
                    target = outs[distance].at[layer]
                    for col in (0, 1):
                        target[parity, half(part), half(col)] = jnp.where(
                            inside, turned[col], turned[col + 1]
                        ).astype(BF)


def transmission_windows(where, offsets, phase, amp):
    shape = jax.ShapeDtypeStruct((2, 2, N, N), BF)
    return pl.pallas_call(
        window_kernel,
        name="windows",
        out_shape=[shape] * RING,
        in_specs=[SM, SM, ANY, ANY],
        out_specs=[VM] * RING,
        scratch_shapes=[
            pltpu.VMEM((2, 2, 3, PATCH, HALF), F32),
            pltpu.VMEM((2, PATCH, PATCH), F32),
            pltpu.VMEM((2, PATCH, PATCH), F32),
            pltpu.SemaphoreType.DMA((2, 2, 3)),
        ],
        compiler_params=pltpu.CompilerParams(vmem_limit_bytes=VMEM_LIMIT),
    )(where, offsets, in_hbm(phase), in_hbm(amp))


def column_pieces(wave, place_at, target):
    width = N // DEPTH
    lane = lax.broadcasted_iota(jnp.int32, (HALF, HALF), 1) // width
    for far in (0, 1):
        value = jnp.zeros((HALF, HALF), F32)
        for parity in (0, 1):
            for part in (0, 1):
                place = 2 * parity + part
                source = wave[parity, half(part), half(far)].astype(F32)
                turn = (place + RING - place_at) % RING * width
                value = jnp.where(lane == place, pltpu.roll(source, turn, 1), value)
        target[:, half(far)] = value.astype(BF)


def chain_kernel(first, where, start, *rest):
    count = RING + 1 if first else RING
    windows = rest[:RING]
    earlier = () if first else rest[RING : 2 * RING]
    rest = rest[RING + len(earlier) :]
    tables = rest[:5]
    outs = rest[5 : 5 + count]
    trans, waves, middle, mixed, filtered, second = rest[5 + count :]
    rank = where[0]
    active = where[1] == 1 if first else where[1] == 0

    @pl.when(active)
    def _():
        for parity in (0, 1):
            waves[(2 * RING - 1 - rank) % RING, parity] = start[parity * N : (parity + 1) * N, :]

        def pair(step, carry):
            pair_at = RING - 1 - step
            slot = (pair_at + RING - rank) % RING
            for k in range(RING):

                @pl.when(slot == k)
                def _(k=k):
                    for parity in (0, 1):
                        outs[k][parity * N : (parity + 1) * N, :] = waves[k, parity]

            source = waves.at[slot]
            target = waves.at[
                jnp.where(pair_at == 0, RING, (pair_at + 2 * RING - 1 - rank) % RING)
            ]
            for layer, begin, end in ((1, source, middle), (0, middle, target)):

                def ready(layer=layer):
                    distance = (rank + RING - pair_at) % RING
                    for k in range(RING):

                        @pl.when(distance == k)
                        def _(k=k):
                            for parity in (0, 1):
                                trans[parity] = windows[k][layer, parity]

                def finish(parity, reals, imags, layer=layer, end=end):
                    for col in (0, 1):
                        tr = trans[parity, half(0), half(col)].astype(F32)
                        ti = trans[parity, half(1), half(col)].astype(F32)
                        qr, qi = reals[col], imags[col]
                        end[parity, half(0), half(col)] = (tr * qr + ti * qi).astype(BF)
                        end[parity, half(1), half(col)] = (tr * qi - ti * qr).astype(BF)

                back_step(begin, tables, mixed, filtered, second, finish, ready)
            return carry

        lax.fori_loop(0, RING, pair, 0)
        if first:
            for parity in (0, 1):
                outs[RING][parity * N : (parity + 1) * N, :] = waves[RING, parity]
        else:
            for k in range(RING):
                column_pieces(waves.at[RING], (rank + k) % RING, outs[k].at[2 * N :])

    if not first:

        @pl.when(jnp.logical_not(active))
        def _():
            for k in range(RING):
                outs[k][: 2 * N, :] = earlier[k][...]
                outs[k][2 * N :, :] = jnp.zeros((HALF, N), BF)


def run_chain(first, where, start, windows, earlier, tables):
    count = RING + 1 if first else RING
    wave = jax.ShapeDtypeStruct((2 * N if first else 2 * N + HALF, N), BF)
    return pl.pallas_call(
        functools.partial(chain_kernel, first),
        name="chain_deep" if first else "chain_top",
        out_shape=[wave] * count,
        in_specs=[SM] + [VM] * (RING + 6 + len(earlier)),
        out_specs=[VM] * count,
        scratch_shapes=[
            pltpu.VMEM((2, N, N), BF),
            pltpu.VMEM((RING + 1, 2, N, N), BF),
            pltpu.VMEM((2, N, N), BF),
            *step_scratch(),
        ],
        compiler_params=pltpu.CompilerParams(vmem_limit_bytes=VMEM_LIMIT),
    )(where, start, *windows, *earlier, *tables)


def visit_kernel(index, where, offsets, entry, window, psi, *rest):
    tables = rest[:5]
    grads, middle, mixed, filtered, second = rest[-5:]
    if index == 0:
        grads[...] = jnp.zeros_like(grads)
    lane = lax.broadcasted_iota(jnp.int32, (HALF, HALF), 1)
    position = (where[0] + RING - index) % RING
    col_at = offsets[position, 1]
    turn = col_at % HALF
    inside = lane >= col_at

    for layer in (1, 0):

        def finish(parity, reals, imags, layer=layer):
            terms = ([], [])
            for col in (0, 1):
                wr = psi[layer, parity, half(0), half(col)].astype(F32)
                wi = psi[layer, parity, half(1), half(col)].astype(F32)
                qr, qi = reals[col], imags[col]
                terms[0].append(pltpu.roll(wr * qr + wi * qi, turn, 1))
                terms[1].append(pltpu.roll(wr * qi - wi * qr, turn, 1))
                if layer == 1:
                    tr = window[layer, parity, half(0), half(col)].astype(F32)
                    ti = window[layer, parity, half(1), half(col)].astype(F32)
                    middle[parity, half(0), half(col)] = (tr * qr + ti * qi).astype(BF)
                    middle[parity, half(1), half(col)] = (tr * qi - ti * qr).astype(BF)
            rows = pl.ds(offsets[position, 0] + parity, HALF, stride=2)
            zero = jnp.zeros((HALF, HALF), F32)
            for part in (0, 1):
                left, right = terms[part]
                placed = (
                    jnp.where(inside, left, zero),
                    jnp.where(inside, right, left),
                    jnp.where(inside, zero, right),
                )
                for col in range(3):
                    grads[layer, part, col, rows, :] += placed[col]

        if layer == 1:
            waves = (entry[:N, :], entry[N : 2 * N, :])
            back_step(waves, tables, mixed, filtered, second, finish)
        else:
            back_step(middle, tables, mixed, filtered, second, finish)


def visit(index, where, offsets, entry, window, psi, tables, grads):
    earlier = () if index == 0 else (grads,)
    return pl.pallas_call(
        functools.partial(visit_kernel, index),
        name=f"visit_{index}",
        out_shape=jax.ShapeDtypeStruct((2, 2, 3, PATCH, HALF), F32),
        in_specs=[SM, SM] + [VM] * (8 + len(earlier)),
        out_specs=VM,
        scratch_shapes=[
            pltpu.VMEM((2, N, N), BF),
            *step_scratch(),
        ],
        input_output_aliases={10: 0} if earlier else {},
        compiler_params=pltpu.CompilerParams(vmem_limit_bytes=VMEM_LIMIT),
    )(where, offsets, entry, window, psi, *tables, *earlier)


def probe_sum_kernel(*refs):
    entries, (own, other) = refs[:RING], refs[RING:]
    total = entries[0][2 * N :, :].astype(F32)
    for entry in entries[1:]:
        total = total + entry[2 * N :, :].astype(F32)
    own[...] = total[:, :HALF].astype(BF)
    other[...] = total[:, HALF:].astype(BF)


def probe_sum(entries):
    shape = jax.ShapeDtypeStruct((HALF, HALF), BF)
    return pl.pallas_call(
        probe_sum_kernel,
        name="probe_sum",
        out_shape=[shape, shape],
        in_specs=[VM] * RING,
        out_specs=[VM, VM],
        compiler_params=pltpu.CompilerParams(vmem_limit_bytes=VMEM_LIMIT),
    )(*entries)


def pack_kernel(where, grads, own_probe, far_probe, keep, send, summed):
    core, y_at = where[2], where[3]

    @pl.when(where[1] == 0)
    def _():
        summed[...] = own_probe[...].astype(F32)

    @pl.when(where[1] == 1)
    def _():
        summed[...] = far_probe[...].astype(F32)

    for distance in range(RING):
        for x_at in (0, 1):
            for out, core_at in ((keep, core), (send, 1 - core)):
                chunk = (x_at * RING + (y_at + distance) % RING) * 2 + core_at
                rows = pl.ds(pl.multiple_of(chunk * EACH, 8), EACH)
                own = pl.ds(pl.multiple_of(chunk * 8, 8), 8)
                for col in range(3):
                    pieces = [
                        grads[layer, part, col, rows, :] for layer in (0, 1) for part in (0, 1)
                    ]
                    pieces.append(summed[own, :] if col == 0 else jnp.zeros((8, HALF), F32))
                    pieces.append(jnp.zeros((8, HALF), F32))
                    out[distance, x_at, :, half(col)] = jnp.concatenate(pieces, 0).astype(BF)


def packed(where, grads, own_probe, far_probe):
    shape = jax.ShapeDtypeStruct((RING, 2, CHUNK, PATCH), BF)
    return pl.pallas_call(
        pack_kernel,
        name="pack",
        out_shape=[shape, shape],
        in_specs=[SM, VM, VM, VM],
        out_specs=[VM, VM],
        scratch_shapes=[pltpu.VMEM((HALF, HALF), F32)],
        compiler_params=pltpu.CompilerParams(vmem_limit_bytes=VMEM_LIMIT),
    )(where, grads, own_probe, far_probe)


def core_sum_kernel(keep, arrived, *outs):
    for distance in range(RING):
        for x_at in (0, 1):
            total = keep[distance, x_at].astype(F32) + arrived[distance, x_at].astype(F32)
            outs[distance][x_at] = total.astype(BF)


def core_sum(keep, arrived):
    return pl.pallas_call(
        core_sum_kernel,
        name="core_sum",
        out_shape=[jax.ShapeDtypeStruct((2, CHUNK, PATCH), BF)] * RING,
        in_specs=[VM, VM],
        out_specs=[VM] * RING,
        compiler_params=pltpu.CompilerParams(vmem_limit_bytes=VMEM_LIMIT),
    )(keep, arrived)


def ring_sum_kernel(where, *rest):
    parts, (keep, send) = rest[:RING], rest[RING:]
    x_at = where[4]
    for out, which in ((keep, x_at), (send, 1 - x_at)):
        total = parts[0][which].astype(F32)
        for part in parts[1:]:
            total = total + part[which].astype(F32)
        out[...] = total.astype(out.dtype)


def ring_sum(where, parts):
    return pl.pallas_call(
        ring_sum_kernel,
        name="ring_sum",
        out_shape=[
            jax.ShapeDtypeStruct((CHUNK, PATCH), F32),
            jax.ShapeDtypeStruct((CHUNK, PATCH), BF),
        ],
        in_specs=[SM] + [VM] * RING,
        out_specs=[VM, VM],
        compiler_params=pltpu.CompilerParams(vmem_limit_bytes=VMEM_LIMIT),
    )(where, *parts)


def last_sum_kernel(keep, arrived, rows_out, probe_out):
    total = keep[...] + arrived[...].astype(F32)
    rows_out[...] = total[: 4 * EACH]
    probe_out[...] = total[4 * EACH : 4 * EACH + 8, :HALF]


def last_sum(keep, arrived):
    return pl.pallas_call(
        last_sum_kernel,
        name="last_sum",
        out_shape=[
            jax.ShapeDtypeStruct((4 * EACH, PATCH), F32),
            jax.ShapeDtypeStruct((8, HALF), F32),
        ],
        compiler_params=pltpu.CompilerParams(vmem_limit_bytes=VMEM_LIMIT),
    )(keep, arrived)


def moved(array, dx, dy, dc):
    route = [
        (8 * x + 2 * y + c, 8 * (x ^ dx) + 2 * ((y + dy) % RING) + (c ^ dc))
        for x in range(2)
        for y in range(RING)
        for c in range(2)
    ]
    return lax.ppermute(array, "probe", route)


def order_kernel(where, residual, saved, start, *rest):
    outs, (first, begin, waves, sems) = rest[:RING], rest[RING:]
    rank = where[0]
    loads = [pltpu.make_async_copy(residual.at[rank], first, sems.at[RING])]
    for index in range(RING):
        position = (rank + RING - index) % RING
        loads.append(
            pltpu.make_async_copy(saved.at[:, position], waves.at[index], sems.at[index])
        )
    for copy in loads:
        copy.start()
    rows = lax.broadcasted_iota(jnp.int32, (N, N), 0)
    cols = lax.broadcasted_iota(jnp.int32, (N, N), 1)
    take = (cols == 2 * (rows % HALF) + rows // HALF).astype(F32).astype(BF)

    def reorder(source, target):
        for part in (0, 1):
            ordered = dot(take, source[part]).astype(BF)
            for parity in (0, 1):
                target[parity, half(part), :] = ordered[half(parity), :]

    loads[0].wait()
    reorder(first, begin)
    for parity in (0, 1):
        start[parity * N : (parity + 1) * N, :] = begin[parity]
    for index in range(RING):
        loads[1 + index].wait()
        for layer in (0, 1):
            reorder(waves.at[index, layer], outs[index].at[layer])


def row_parity_first(where, residual, saved):
    wave = (2, N, N)
    return pl.pallas_call(
        order_kernel,
        name="reorder",
        out_shape=[jax.ShapeDtypeStruct((2 * N, N), BF)]
        + [jax.ShapeDtypeStruct((2, *wave), BF)] * RING,
        in_specs=[SM, ANY, ANY],
        out_specs=[VM] * (RING + 1),
        scratch_shapes=[
            pltpu.VMEM(wave, BF),
            pltpu.VMEM(wave, BF),
            pltpu.VMEM((RING, 2, *wave), BF),
            pltpu.SemaphoreType.DMA((RING + 1,)),
        ],
        compiler_params=pltpu.CompilerParams(vmem_limit_bytes=VMEM_LIMIT),
    )(where, in_hbm(residual), in_hbm(saved))


def turned(array, distance):
    route = [
        (RING * ring + i, RING * ring + (i + distance) % RING)
        for ring in range(2)
        for i in range(RING)
    ]
    return lax.ppermute(array, "depth", route)


def exchanged(arrays):
    return [arrays[0]] + [turned(arrays[k], k) for k in range(1, RING)]


def shards(residual, saved_waves, object_phase, object_amp, prop_phase, offsets):
    depth_at = lax.axis_index("depth")
    probe_at = lax.axis_index("probe")
    where = jnp.stack(
        [depth_at % RING, depth_at // RING, probe_at % 2, probe_at // 2 % RING, probe_at // 8]
    ).astype(jnp.int32)
    own = transmission_windows(where, offsets, object_phase, object_amp)
    tables = filters(prop_phase)
    start, *waves = row_parity_first(where, residual, saved_waves)
    foreign = exchanged(own)
    *deep, leaving = run_chain(True, where, start, foreign, (), tables)
    arrived = lax.ppermute(leaving, "depth", [(RING + i, i) for i in range(RING)])
    entries = exchanged(run_chain(False, where, arrived, foreign, deep, tables))
    grads = None
    for index in (0, 3, 1, 2):
        if index == 2:
            *entries, grads = lax.optimization_barrier((*entries, grads))
            own_probe, other_probe = probe_sum(entries)
            far_probe = lax.ppermute(other_probe, "depth", [(i, RING + i) for i in range(RING)])
        window = own[(RING - index) % RING]
        grads = visit(
            index, where, offsets, entries[index], window, waves[index], tables, grads
        )
    keep, send = packed(where, grads, own_probe, far_probe)
    parts = list(core_sum(keep, moved(send, 0, 0, 1)))
    parts = parts[:1] + [moved(parts[k], 0, k, 0) for k in range(1, RING)]
    keep, send = ring_sum(where, parts)
    rows, probe_rows = last_sum(keep, moved(send, 1, 0, 0))
    object_grad = rows.reshape(2, 2, EACH, PATCH)
    probe_grad = probe_rows.reshape(8, 2, 2, N // DEPTH).transpose(2, 0, 1, 3)
    return (object_grad, probe_grad.reshape(2, 16, N // DEPTH))


def solution(mesh):
    return jax.shard_map(
        shards,
        mesh=mesh,
        in_specs=(
            P("probe", None, None, None),
            P("depth", "probe", None, None, None),
            P("depth", None, None),
            P("depth", None, None),
            P(),
            P("probe", None),
        ),
        out_specs=(P("depth", None, "probe", None), P(None, "probe", "depth")),
        check_vma=False,
    )
```

```python
import functools
import math

import jax
import jax.numpy as jnp
from jax import lax
from jax.experimental import pallas as pl
from jax.experimental.pallas import tpu as pltpu
from jax.sharding import PartitionSpec as P

BF = jnp.bfloat16
F32 = jnp.float32
RING = 4
DEPTH = 8
N = 256
HALF = 128
PATCH = 384
EACH = PATCH // 16
CHUNK = 4 * EACH + 16
ANY = pl.BlockSpec(memory_space=pl.ANY)
VM = pl.BlockSpec(memory_space=pltpu.VMEM)
SM = pl.BlockSpec(memory_space=pltpu.SMEM)
SINE = (0.999999995716, -0.166666579699, 0.00833305061733, -0.000198090463574, 2.60516627618e-06)
COSINE = (0.99999999978, -0.49999999357, 0.0416666362089, -0.00138883608423, 2.47601355058e-05, -2.60510761786e-07)
VMEM_LIMIT = 20 * 1024 * 1024


def in_hbm(array):
    return pltpu.with_memory_space_constraint(array, pltpu.HBM)


def half(index):
    return slice(index * HALF, (index + 1) * HALF)


def dot(a, b):
    return jnp.dot(a, b, preferred_element_type=F32)


def back_step(source, tables, mixed, filtered, second, finish):
    inward, table, flipped, kernel_cos, kernel_sin = tables
    for part in (0, 1):
        even = dot(inward[0, half(part), :], source[0])
        odd = dot(inward[1, half(part), :], source[1])
        for row, value in ((0, even + odd), (1, even - odd)):
            left, right = value[:, :HALF], value[:, HALF:]
            mixed[0, half(row), half(part)] = (left + right).astype(BF)
            mixed[1, half(row), half(part)] = (left - right).astype(BF)
    for col in (0, 1):
        upper = dot(mixed[col, half(0), :], flipped[col])
        lower = dot(mixed[col, half(1), :], flipped[col])
        for parity in (0, 1):
            real = upper[:, half(parity)]
            imag = lower[:, half(parity)]
            kc = kernel_cos[half(parity), half(col)]
            ks = kernel_sin[half(parity), half(col)]
            filtered[parity, half(0), half(col)] = (kc * real + ks * imag).astype(BF)
            filtered[parity, half(1), half(col)] = (kc * imag - ks * real).astype(BF)
    for part in (0, 1):
        even = dot(flipped[0, half(part), :], filtered[0])
        odd = dot(flipped[1, half(part), :], filtered[1])
        total = (even + odd).astype(BF)
        diff = (even - odd).astype(BF)
        for col in (0, 1):
            second[col, half(0), half(part)] = total[:, half(col)]
            second[col, half(1), half(part)] = diff[:, half(col)]
    totals, diffs = [], []
    for row in (0, 1):
        even = dot(second[0, half(row), :], table[0])
        odd = dot(second[1, half(row), :], table[1])
        totals.append(even + odd)
        diffs.append(even - odd)
    for parity in (0, 1):
        finish(
            parity,
            (totals[0][:, half(parity)], diffs[0][:, half(parity)]),
            (totals[1][:, half(parity)], diffs[1][:, half(parity)]),
        )


def step_scratch():
    return [pltpu.VMEM((2, N, N), BF), pltpu.VMEM((2, N, N), BF), pltpu.VMEM((2, N, N), BF)]


def sine_and_cosine(angle):
    half_angle = 0.5 * angle
    square = half_angle * half_angle

    def series(factors):
        value = jnp.full_like(square, factors[-1])
        for factor in factors[-2::-1]:
            value = value * square + factor
        return value

    low_sine = half_angle * series(SINE)
    low_cosine = series(COSINE)
    return 2.0 * low_sine * low_cosine, 1.0 - 2.0 * low_sine * low_sine


def write_tables(inward, table, flipped):
    first = lax.broadcasted_iota(jnp.int32, (HALF, HALF), 0)
    second = lax.broadcasted_iota(jnp.int32, (HALF, HALF), 1)
    factor = 1.0 / math.sqrt(N)
    for spread, other, targets in (
        (second, first, ((inward, 1.0), (flipped, -1.0))),
        (first, second, ((table, 1.0),)),
    ):
        for parity in (0, 1):
            order = (2 * spread + parity) * other % N
            order = jnp.where(order > HALF, order - N, order)
            sine, cosine = sine_and_cosine(2.0 * math.pi / N * order.astype(F32))
            for target, sign in targets:
                for row in (0, 1):
                    target[parity, half(row), half(row)] = (cosine * factor).astype(BF)
                    turned_sine = sine * (factor * (sign if row == 0 else -sign))
                    target[parity, half(row), half(1 - row)] = turned_sine.astype(BF)


def filter_kernel(phase, inward, table, flipped, kernel_cos, kernel_sin, plain):
    write_tables(inward, table, flipped)
    rows = lax.broadcasted_iota(jnp.int32, (N, N), 0)
    cols = lax.broadcasted_iota(jnp.int32, (N, N), 1)
    take = (rows == 2 * (cols % HALF) + cols // HALF).astype(F32).astype(BF)
    for col in (0, 1):
        sine, cosine = sine_and_cosine(phase[:, half(col)])
        plain[0, col] = cosine
        plain[1, col] = sine
    for index, out in ((0, kernel_cos), (1, kernel_sin)):
        for parity in (0, 1):
            picked = [plain[index, col, pl.ds(parity, HALF, stride=2), :] for col in (0, 1)]
            rest = jnp.concatenate(picked, 1)
            value = jnp.zeros((HALF, N), F32)
            for _ in range(3):
                term = rest.astype(BF)
                value = value + dot(term, take)
                rest = rest - term.astype(F32)
            out[half(parity), :] = value


def filters(phase):
    shape = jax.ShapeDtypeStruct((N, N), F32)
    pair = jax.ShapeDtypeStruct((2, N, N), BF)
    return pl.pallas_call(
        filter_kernel,
        name="filters",
        out_shape=[pair, pair, pair, shape, shape],
        in_specs=[VM],
        out_specs=[VM] * 5,
        scratch_shapes=[pltpu.VMEM((2, 2, N, HALF), F32)],
        compiler_params=pltpu.CompilerParams(vmem_limit_bytes=VMEM_LIMIT),
    )(phase)


def window_kernel(where, offsets, phase_all, amp_all, *rest):
    outs, (field, phase, amp, sems) = rest[:RING], rest[RING:]
    rank = where[0]

    def loads(layer, block):
        rows = half(block)
        return [
            pltpu.make_async_copy(
                source.at[layer, rows, :], target.at[layer, rows, :], sems.at[kind, layer, block]
            )
            for kind, source, target in ((0, phase_all, phase), (1, amp_all, amp))
        ]

    for layer in (0, 1):
        for block in range(3):
            for copy in loads(layer, block):
                copy.start()
    for layer in (0, 1):
        for block in range(3):
            for copy in loads(layer, block):
                copy.wait()
            for col in range(3):
                sine, cosine = sine_and_cosine(phase[layer, half(block), half(col)])
                size = amp[layer, half(block), half(col)]
                field[layer, 0, col, half(block), :] = size * cosine
                field[layer, 1, col, half(block), :] = size * sine
    lane = lax.broadcasted_iota(jnp.int32, (HALF, HALF), 1)
    for distance in range(RING):
        position = (rank + distance) % RING
        col_at = offsets[position, 1]
        turn = (HALF - col_at) % HALF
        inside = lane < HALF - col_at
        for parity in (0, 1):
            rows = pl.ds(offsets[position, 0] + parity, HALF, stride=2)
            for layer in (0, 1):
                for part in (0, 1):
                    turned = [
                        pltpu.roll(field[layer, part, col, rows, :], turn, 1) for col in range(3)
                    ]
                    target = outs[distance].at[layer]
                    for col in (0, 1):
                        target[parity, half(part), half(col)] = jnp.where(
                            inside, turned[col], turned[col + 1]
                        ).astype(BF)


def transmission_windows(where, offsets, phase, amp):
    shape = jax.ShapeDtypeStruct((2, 2, N, N), BF)
    return pl.pallas_call(
        window_kernel,
        name="windows",
        out_shape=[shape] * RING,
        in_specs=[SM, SM, ANY, ANY],
        out_specs=[VM] * RING,
        scratch_shapes=[
            pltpu.VMEM((2, 2, 3, PATCH, HALF), F32),
            pltpu.VMEM((2, PATCH, PATCH), F32),
            pltpu.VMEM((2, PATCH, PATCH), F32),
            pltpu.SemaphoreType.DMA((2, 2, 3)),
        ],
        compiler_params=pltpu.CompilerParams(vmem_limit_bytes=VMEM_LIMIT),
    )(where, offsets, in_hbm(phase), in_hbm(amp))


def column_pieces(wave, place_at, target):
    width = N // DEPTH
    lane = lax.broadcasted_iota(jnp.int32, (HALF, HALF), 1) // width
    for far in (0, 1):
        value = jnp.zeros((HALF, HALF), F32)
        for parity in (0, 1):
            for part in (0, 1):
                place = 2 * parity + part
                source = wave[parity, half(part), half(far)].astype(F32)
                turn = (place + RING - place_at) % RING * width
                value = jnp.where(lane == place, pltpu.roll(source, turn, 1), value)
        target[:, half(far)] = value.astype(BF)


def chain_kernel(first, where, start, *rest):
    count = RING + 1 if first else RING
    windows = rest[:RING]
    earlier = () if first else rest[RING : 2 * RING]
    rest = rest[RING + len(earlier) :]
    tables = rest[:5]
    outs = rest[5 : 5 + count]
    trans, waves, middle, mixed, filtered, second = rest[5 + count :]
    rank = where[0]
    active = where[1] == 1 if first else where[1] == 0

    @pl.when(active)
    def _():
        for parity in (0, 1):
            waves[(2 * RING - 1 - rank) % RING, parity] = start[parity * N : (parity + 1) * N, :]

        def pair(step, carry):
            pair_at = RING - 1 - step
            slot = (pair_at + RING - rank) % RING
            for k in range(RING):

                @pl.when(slot == k)
                def _(k=k):
                    for parity in (0, 1):
                        outs[k][parity * N : (parity + 1) * N, :] = waves[k, parity]
                    trans[...] = windows[(RING - k) % RING][...]

            source = waves.at[slot]
            target = waves.at[
                jnp.where(pair_at == 0, RING, (pair_at + 2 * RING - 1 - rank) % RING)
            ]
            for layer, begin, end in ((1, source, middle), (0, middle, target)):

                def finish(parity, reals, imags, layer=layer, end=end):
                    for col in (0, 1):
                        tr = trans[layer, parity, half(0), half(col)].astype(F32)
                        ti = trans[layer, parity, half(1), half(col)].astype(F32)
                        qr, qi = reals[col], imags[col]
                        end[parity, half(0), half(col)] = (tr * qr + ti * qi).astype(BF)
                        end[parity, half(1), half(col)] = (tr * qi - ti * qr).astype(BF)

                back_step(begin, tables, mixed, filtered, second, finish)
            return carry

        lax.fori_loop(0, RING, pair, 0)
        if first:
            for parity in (0, 1):
                outs[RING][parity * N : (parity + 1) * N, :] = waves[RING, parity]
        else:
            for k in range(RING):
                column_pieces(waves.at[RING], (rank + k) % RING, outs[k].at[2 * N :])

    if not first:

        @pl.when(jnp.logical_not(active))
        def _():
            for k in range(RING):
                outs[k][: 2 * N, :] = earlier[k][...]
                outs[k][2 * N :, :] = jnp.zeros((HALF, N), BF)


def run_chain(first, where, start, windows, earlier, tables):
    count = RING + 1 if first else RING
    wave = jax.ShapeDtypeStruct((2 * N if first else 2 * N + HALF, N), BF)
    return pl.pallas_call(
        functools.partial(chain_kernel, first),
        name="chain_deep" if first else "chain_top",
        out_shape=[wave] * count,
        in_specs=[SM] + [VM] * (RING + 6 + len(earlier)),
        out_specs=[VM] * count,
        scratch_shapes=[
            pltpu.VMEM((2, 2, N, N), BF),
            pltpu.VMEM((RING + 1, 2, N, N), BF),
            pltpu.VMEM((2, N, N), BF),
            *step_scratch(),
        ],
        compiler_params=pltpu.CompilerParams(vmem_limit_bytes=VMEM_LIMIT),
    )(where, start, *windows, *earlier, *tables)


def visit_kernel(index, where, offsets, entry, window, psi, *rest):
    tables = rest[:5]
    grads, middle, mixed, filtered, second = rest[-5:]
    if index == 0:
        grads[...] = jnp.zeros_like(grads)
    lane = lax.broadcasted_iota(jnp.int32, (HALF, HALF), 1)
    position = (where[0] + RING - index) % RING
    col_at = offsets[position, 1]
    turn = col_at % HALF
    inside = lane >= col_at

    for layer in (1, 0):

        def finish(parity, reals, imags, layer=layer):
            terms = ([], [])
            for col in (0, 1):
                wr = psi[layer, parity, half(0), half(col)].astype(F32)
                wi = psi[layer, parity, half(1), half(col)].astype(F32)
                qr, qi = reals[col], imags[col]
                terms[0].append(pltpu.roll(wr * qr + wi * qi, turn, 1))
                terms[1].append(pltpu.roll(wr * qi - wi * qr, turn, 1))
                if layer == 1:
                    tr = window[layer, parity, half(0), half(col)].astype(F32)
                    ti = window[layer, parity, half(1), half(col)].astype(F32)
                    middle[parity, half(0), half(col)] = (tr * qr + ti * qi).astype(BF)
                    middle[parity, half(1), half(col)] = (tr * qi - ti * qr).astype(BF)
            rows = pl.ds(offsets[position, 0] + parity, HALF, stride=2)
            zero = jnp.zeros((HALF, HALF), F32)
            for part in (0, 1):
                left, right = terms[part]
                placed = (
                    jnp.where(inside, left, zero),
                    jnp.where(inside, right, left),
                    jnp.where(inside, zero, right),
                )
                for col in range(3):
                    grads[layer, part, col, rows, :] += placed[col]

        if layer == 1:
            waves = (entry[:N, :], entry[N : 2 * N, :])
            back_step(waves, tables, mixed, filtered, second, finish)
        else:
            back_step(middle, tables, mixed, filtered, second, finish)


def visit(index, where, offsets, entry, window, psi, tables, grads):
    earlier = () if index == 0 else (grads,)
    return pl.pallas_call(
        functools.partial(visit_kernel, index),
        name=f"visit_{index}",
        out_shape=jax.ShapeDtypeStruct((2, 2, 3, PATCH, HALF), F32),
        in_specs=[SM, SM] + [VM] * (8 + len(earlier)),
        out_specs=VM,
        scratch_shapes=[
            pltpu.VMEM((2, N, N), BF),
            *step_scratch(),
        ],
        input_output_aliases={10: 0} if earlier else {},
        compiler_params=pltpu.CompilerParams(vmem_limit_bytes=VMEM_LIMIT),
    )(where, offsets, entry, window, psi, *tables, *earlier)


def probe_sum_kernel(*refs):
    entries, (own, other) = refs[:RING], refs[RING:]
    total = entries[0][2 * N :, :].astype(F32)
    for entry in entries[1:]:
        total = total + entry[2 * N :, :].astype(F32)
    own[...] = total[:, :HALF].astype(BF)
    other[...] = total[:, HALF:].astype(BF)


def probe_sum(entries):
    shape = jax.ShapeDtypeStruct((HALF, HALF), BF)
    return pl.pallas_call(
        probe_sum_kernel,
        name="probe_sum",
        out_shape=[shape, shape],
        in_specs=[VM] * RING,
        out_specs=[VM, VM],
        compiler_params=pltpu.CompilerParams(vmem_limit_bytes=VMEM_LIMIT),
    )(*entries)


def pack_kernel(where, grads, own_probe, far_probe, keep, send, summed):
    core, y_at = where[2], where[3]

    @pl.when(where[1] == 0)
    def _():
        summed[...] = own_probe[...].astype(F32)

    @pl.when(where[1] == 1)
    def _():
        summed[...] = far_probe[...].astype(F32)

    for distance in range(RING):
        for x_at in (0, 1):
            for out, core_at in ((keep, core), (send, 1 - core)):
                chunk = (x_at * RING + (y_at + distance) % RING) * 2 + core_at
                rows = pl.ds(pl.multiple_of(chunk * EACH, 8), EACH)
                own = pl.ds(pl.multiple_of(chunk * 8, 8), 8)
                for col in range(3):
                    pieces = [
                        grads[layer, part, col, rows, :] for layer in (0, 1) for part in (0, 1)
                    ]
                    pieces.append(summed[own, :] if col == 0 else jnp.zeros((8, HALF), F32))
                    pieces.append(jnp.zeros((8, HALF), F32))
                    out[distance, x_at, :, half(col)] = jnp.concatenate(pieces, 0).astype(BF)


def packed(where, grads, own_probe, far_probe):
    shape = jax.ShapeDtypeStruct((RING, 2, CHUNK, PATCH), BF)
    return pl.pallas_call(
        pack_kernel,
        name="pack",
        out_shape=[shape, shape],
        in_specs=[SM, VM, VM, VM],
        out_specs=[VM, VM],
        scratch_shapes=[pltpu.VMEM((HALF, HALF), F32)],
        compiler_params=pltpu.CompilerParams(vmem_limit_bytes=VMEM_LIMIT),
    )(where, grads, own_probe, far_probe)


def core_sum_kernel(keep, arrived, *outs):
    for distance in range(RING):
        for x_at in (0, 1):
            total = keep[distance, x_at].astype(F32) + arrived[distance, x_at].astype(F32)
            outs[distance][x_at] = total.astype(BF)


def core_sum(keep, arrived):
    return pl.pallas_call(
        core_sum_kernel,
        name="core_sum",
        out_shape=[jax.ShapeDtypeStruct((2, CHUNK, PATCH), BF)] * RING,
        in_specs=[VM, VM],
        out_specs=[VM] * RING,
        compiler_params=pltpu.CompilerParams(vmem_limit_bytes=VMEM_LIMIT),
    )(keep, arrived)


def ring_sum_kernel(where, *rest):
    parts, (keep, send) = rest[:RING], rest[RING:]
    x_at = where[4]
    for out, which in ((keep, x_at), (send, 1 - x_at)):
        total = parts[0][which].astype(F32)
        for part in parts[1:]:
            total = total + part[which].astype(F32)
        out[...] = total.astype(out.dtype)


def ring_sum(where, parts):
    return pl.pallas_call(
        ring_sum_kernel,
        name="ring_sum",
        out_shape=[
            jax.ShapeDtypeStruct((CHUNK, PATCH), F32),
            jax.ShapeDtypeStruct((CHUNK, PATCH), BF),
        ],
        in_specs=[SM] + [VM] * RING,
        out_specs=[VM, VM],
        compiler_params=pltpu.CompilerParams(vmem_limit_bytes=VMEM_LIMIT),
    )(where, *parts)


def last_sum_kernel(keep, arrived, rows_out, probe_out):
    total = keep[...] + arrived[...].astype(F32)
    rows_out[...] = total[: 4 * EACH]
    probe_out[...] = total[4 * EACH : 4 * EACH + 8, :HALF]


def last_sum(keep, arrived):
    return pl.pallas_call(
        last_sum_kernel,
        name="last_sum",
        out_shape=[
            jax.ShapeDtypeStruct((4 * EACH, PATCH), F32),
            jax.ShapeDtypeStruct((8, HALF), F32),
        ],
        compiler_params=pltpu.CompilerParams(vmem_limit_bytes=VMEM_LIMIT),
    )(keep, arrived)


def moved(array, dx, dy, dc):
    route = [
        (8 * x + 2 * y + c, 8 * (x ^ dx) + 2 * ((y + dy) % RING) + (c ^ dc))
        for x in range(2)
        for y in range(RING)
        for c in range(2)
    ]
    return lax.ppermute(array, "probe", route)


def order_kernel(where, residual, saved, start, *rest):
    outs, (first, begin, waves, sems) = rest[:RING], rest[RING:]
    rank = where[0]
    loads = [pltpu.make_async_copy(residual.at[rank], first, sems.at[RING])]
    for index in range(RING):
        position = (rank + RING - index) % RING
        loads.append(
            pltpu.make_async_copy(saved.at[:, position], waves.at[index], sems.at[index])
        )
    for copy in loads:
        copy.start()
    rows = lax.broadcasted_iota(jnp.int32, (N, N), 0)
    cols = lax.broadcasted_iota(jnp.int32, (N, N), 1)
    take = (cols == 2 * (rows % HALF) + rows // HALF).astype(F32).astype(BF)

    def reorder(source, target):
        for part in (0, 1):
            ordered = dot(take, source[part]).astype(BF)
            for parity in (0, 1):
                target[parity, half(part), :] = ordered[half(parity), :]

    loads[0].wait()
    reorder(first, begin)
    for parity in (0, 1):
        start[parity * N : (parity + 1) * N, :] = begin[parity]
    for index in range(RING):
        loads[1 + index].wait()
        for layer in (0, 1):
            reorder(waves.at[index, layer], outs[index].at[layer])


def row_parity_first(where, residual, saved):
    wave = (2, N, N)
    return pl.pallas_call(
        order_kernel,
        name="reorder",
        out_shape=[jax.ShapeDtypeStruct((2 * N, N), BF)]
        + [jax.ShapeDtypeStruct((2, *wave), BF)] * RING,
        in_specs=[SM, ANY, ANY],
        out_specs=[VM] * (RING + 1),
        scratch_shapes=[
            pltpu.VMEM(wave, BF),
            pltpu.VMEM(wave, BF),
            pltpu.VMEM((RING, 2, *wave), BF),
            pltpu.SemaphoreType.DMA((RING + 1,)),
        ],
        compiler_params=pltpu.CompilerParams(vmem_limit_bytes=VMEM_LIMIT),
    )(where, in_hbm(residual), in_hbm(saved))


def turned(array, distance):
    route = [
        (RING * ring + i, RING * ring + (i + distance) % RING)
        for ring in range(2)
        for i in range(RING)
    ]
    return lax.ppermute(array, "depth", route)


def exchanged(arrays):
    return [arrays[0]] + [turned(arrays[k], k) for k in range(1, RING)]


def shards(residual, saved_waves, object_phase, object_amp, prop_phase, offsets):
    depth_at = lax.axis_index("depth")
    probe_at = lax.axis_index("probe")
    where = jnp.stack(
        [depth_at % RING, depth_at // RING, probe_at % 2, probe_at // 2 % RING, probe_at // 8]
    ).astype(jnp.int32)
    own = transmission_windows(where, offsets, object_phase, object_amp)
    tables = filters(prop_phase)
    start, *waves = row_parity_first(where, residual, saved_waves)
    foreign = exchanged(own)
    *deep, leaving = run_chain(True, where, start, foreign, (), tables)
    arrived = lax.ppermute(leaving, "depth", [(RING + i, i) for i in range(RING)])
    entries = exchanged(run_chain(False, where, arrived, foreign, deep, tables))
    grads = None
    for index in (0, 3, 1, 2):
        if index == 2:
            *entries, grads = lax.optimization_barrier((*entries, grads))
            own_probe, other_probe = probe_sum(entries)
            far_probe = lax.ppermute(other_probe, "depth", [(i, RING + i) for i in range(RING)])
        window = own[(RING - index) % RING]
        grads = visit(
            index, where, offsets, entries[index], window, waves[index], tables, grads
        )
    keep, send = packed(where, grads, own_probe, far_probe)
    parts = list(core_sum(keep, moved(send, 0, 0, 1)))
    parts = parts[:1] + [moved(parts[k], 0, k, 0) for k in range(1, RING)]
    keep, send = ring_sum(where, parts)
    rows, probe_rows = last_sum(keep, moved(send, 1, 0, 0))
    object_grad = rows.reshape(2, 2, EACH, PATCH)
    probe_grad = probe_rows.reshape(8, 2, 2, N // DEPTH).transpose(2, 0, 1, 3)
    return (object_grad, probe_grad.reshape(2, 16, N // DEPTH))


def solution(mesh):
    return jax.shard_map(
        shards,
        mesh=mesh,
        in_specs=(
            P("probe", None, None, None),
            P("depth", "probe", None, None, None),
            P("depth", None, None),
            P("depth", None, None),
            P(),
            P("probe", None),
        ),
        out_specs=(P("depth", None, "probe", None), P(None, "probe", "depth")),
        check_vma=False,
    )
```
